32 devices in a mesh: dp: 4 (over y, core), ctx: 8 (over z, x).
Axes of the slice: x: 2, y: 2, z: 4, core: 2. Of those that a mesh axis runs over, the one named last changes fastest.
Arguments:
- queries: bfloat16 [4096, 2048], P(('dp', 'ctx')), may hold values from -6 to 6
- key_rows: bfloat16 [4096, 2048], P(('dp', 'ctx')), may hold values from -6 to 6
- value_rows: bfloat16 [4096, 2048], P(('dp', 'ctx')), may hold values from -6 to 6
- hidden_in: bfloat16 [4096, 2304], P(('dp', 'ctx')), may hold values from -6 to 6
- beta_weight: bfloat16 [2304, 16], replicated, may hold values from -0.125 to 0.125
- log_gate: float32 [16, 4096], P(None, ('dp', 'ctx')), may hold values from -1 to 0
- out_grad: bfloat16 [4096, 2048], P(('dp', 'ctx')), may hold values from -24 to 24
- lengths: int32 [4, 4], P('dp'), may hold values from 1 to 512, 1024 in all within a row
- rewards: float32 [16], replicated, may hold values from -6 to 6
- prompts: int32 [16], replicated, may hold values from 0 to 3
Outputs:
- query_grad: bfloat16 [4096, 2048], P(('dp', 'ctx'))
- key_grad: bfloat16 [4096, 2048], P(('dp', 'ctx'))
- value_grad: bfloat16 [4096, 2048], P(('dp', 'ctx'))
- gate_grad: float32 [16, 4096], P(None, ('dp', 'ctx'))
- beta_weight_grad: float32 [2304, 16], P(('dp', 'ctx'))
The draws below stay inside these ranges and needn't reach their ends.
Inputs may be any that keep to these rules, and one draw needn't show every extreme that they name: `lengths`: each row sums to 1024; its largest entry is exactly 512.
All inputs are finite; a program needn't handle non-finite values.
Results may differ from the reference program's by a relative error of at most 0.001.
Values sent between devices are 32-bit elements; how exact they have to be, the bound alone decides.
A program may use at most 128 MiB of HBM per device.

```python
import math
import jax
import jax.numpy as jnp
import numpy as np
from jax import lax

D = 2304
HALF_HEADS = 16
HEAD_DIM = 128
BLOCK = 64
TOK_DEV = 128
ROLL = 4
GROUP_TOKENS = 1024
TOTAL_TOKENS = 4096
ROLLOUTS = 16
PROMPTS = 4
N_DP = 4


def draw_log_gate(key, part):
    key_vectors = jax.random.split(key, 7)
    fast_share = 0.5
    fast = jax.random.uniform(key_vectors[0], (HALF_HEADS, 1)) < fast_share
    fast_rate = jnp.exp(jax.random.uniform(key_vectors[1], (HALF_HEADS, 1), minval=math.log(1.0 / 50.0), maxval=math.log(1.0 / 30.0)))
    slow_rate = jnp.exp(jax.random.uniform(key_vectors[2], (HALF_HEADS, 1), minval=math.log(0.05), maxval=math.log(0.3))) / GROUP_TOKENS
    decay_speed = jnp.where(fast, fast_rate, slow_rate)
    block_multiplier = jnp.exp(jax.random.uniform(key_vectors[3], (HALF_HEADS, TOTAL_TOKENS // TOK_DEV, 1), minval=math.log(0.5), maxval=math.log(2.0)))
    block_multiplier = jnp.broadcast_to(block_multiplier, (HALF_HEADS, TOTAL_TOKENS // TOK_DEV, TOK_DEV)).reshape(HALF_HEADS, TOTAL_TOKENS)
    token_multiplier = jnp.exp(jax.random.uniform(key_vectors[4], (HALF_HEADS, TOTAL_TOKENS), minval=math.log(0.5), maxval=math.log(2.0)))
    spike_position = jax.random.uniform(key_vectors[5], (1, TOTAL_TOKENS)) < 3.0 / GROUP_TOKENS
    spike_magnitude = jax.random.uniform(key_vectors[6], (HALF_HEADS, TOTAL_TOKENS), minval=math.log(0.5), maxval=math.log(0.8))
    return (-decay_speed * block_multiplier * token_multiplier + jnp.where(spike_position, spike_magnitude, 0.0)).astype(jnp.float32)


def plant(entries, own_key, low, high):
    longest = entries.shape.index(max(entries.shape))
    spots = []
    for shift in (0, 1):
        where = [jax.random.randint(jax.random.fold_in(own_key, axis), (), 0, length) for axis, length in enumerate(entries.shape)]
        where[longest] = (where[longest] + shift) % entries.shape[longest]
        spots.append(tuple(where))
    return entries.at[spots[0]].set(low).at[spots[1]].set(high)


def with_spikes(array, key, source, target, shards_of, factor):
    owner, partner = [(jnp.arange(array.shape[position]) // (array.shape[position] // shards_of)).reshape([-1 if axis == position else 1 for axis in range(array.ndim)]) for position in (source, target)]
    chosen = jax.random.permutation(key, shards_of)[partner]
    strong = (owner == chosen) | (owner == (partner + shards_of // 2) % shards_of)
    return jnp.where(strong, factor * array, array)


def block_levels(stream_key, shape, cuts, low, high):
    loudness, own = 1.0, jax.random.fold_in(stream_key, 6)
    for position, shards_of in cuts:
        heights = jnp.exp(jax.random.uniform(jax.random.fold_in(own, position), (shards_of,), jnp.float32, low / len(cuts), high / len(cuts)))
        loudness = loudness * jnp.repeat(heights, shape[position] // shards_of).reshape([-1 if axis == position else 1 for axis in range(len(shape))])
    return loudness


def split_up(count, total, bound, skew):
    weights = [(1 << 20) // math.isqrt(rank ** skew) + 1 for rank in range(2, count + 1)]
    surplus, holding = total - bound - (count - 1), [1] * (count - 1)
    while surplus > 0:
        movable = [i for i in range(count - 1) if holding[i] < bound]
        pool, left = sum([weights[i] for i in movable]), surplus
        for i in movable:
            extra = min(bound - holding[i], max(1, left * weights[i] // pool), surplus)
            holding[i] = holding[i] + extra
            surplus = surplus - extra
    return np.array([bound] + holding)


def ragged(own_key, number_of, total, limit, lean):
    if number_of == 2:
        one = jax.random.randint(own_key, (), max(1, total - limit), min(limit, total - 1) + 1)
        return jnp.stack([one, total - one])
    sizes = jnp.asarray(split_up(number_of, total, limit, lean), jnp.int32)
    twos = (number_of - 1) // 2
    donor, taker = sizes[1:1 + 2 * twos:2], sizes[2:2 + 2 * twos:2]
    slack = jnp.minimum(donor - 1, limit - taker)
    shifted = jax.random.randint(jax.random.fold_in(own_key, 1), (twos,), 0, 1 << 20) % (slack + 1)
    sizes = sizes.at[1:1 + 2 * twos:2].set(donor - shifted).at[2:2 + 2 * twos:2].set(taker + shifted)
    return sizes[jax.random.permutation(jax.random.fold_in(own_key, 2), number_of)]


def gaussian(key, dims, scale, reach, cuts=(), held_as=jnp.bfloat16):
    drawn = jax.random.normal(key, dims, jnp.float32) * scale
    if len(cuts) > 0:
        drawn = block_levels(key, dims, cuts, -0.22, 0.18) * drawn
    return jnp.clip(drawn, min=-reach, max=reach).astype(held_as)


def bell_draw_with(rng, shape, scale, reach, cuts, heavy, kind=jnp.bfloat16):
    values = scale * jax.random.normal(rng, shape, jnp.float32)
    if cuts:
        values = values * block_levels(rng, shape, cuts, -0.22, 0.18)
    return jnp.clip(with_spikes(values, jax.random.fold_in(rng, 3), *heavy), -reach, reach).astype(kind)


def setup_inputs(seed: int = 0) -> dict:
    seeds = jax.random.split(jax.random.key(seed), 11)
    return {
        "queries": gaussian(seeds[0], (TOTAL_TOKENS, HALF_HEADS * HEAD_DIM), 1.0, 6.0, ((0, 32),)),
        "key_rows": gaussian(seeds[1], (TOTAL_TOKENS, HALF_HEADS * HEAD_DIM), 1.0, 6.0, ((0, 32),)),
        "value_rows": gaussian(seeds[2], (TOTAL_TOKENS, HALF_HEADS * HEAD_DIM), 1.0, 6.0, ((0, 32),)),
        "hidden_in": bell_draw_with(seeds[3], (TOTAL_TOKENS, D), 1.0, 6.0, ((0, 32),), (0, 1, 32, 2.75)),
        "beta_weight": gaussian(seeds[4], (D, HALF_HEADS), D ** -0.5, 0.125),
        "log_gate": draw_log_gate(jax.random.fold_in(seeds[10], 71), 0),
        "out_grad": gaussian(seeds[6], (TOTAL_TOKENS, HALF_HEADS * HEAD_DIM), 4.0, 24.0, ((0, 32),)),
        "lengths": jax.vmap(lambda own: ragged(own, ROLL, GROUP_TOKENS, GROUP_TOKENS // 2, 2))(jax.random.split(seeds[7], N_DP)).reshape((N_DP, ROLL)).astype(jnp.int32),
        "rewards": gaussian(seeds[8], (ROLLOUTS,), 1.0, 6.0, (), jnp.float32),
        "prompts": plant(jax.random.randint(seeds[9], (ROLLOUTS,), 0, PROMPTS), jax.random.fold_in(seeds[9], 1), 0, PROMPTS - 1).astype(jnp.int32),
    }


highest = lax.Precision.HIGHEST

def unit_rows(rows):
    return rows * lax.rsqrt(lax.optimization_barrier(jnp.sum(rows * rows, axis=-1, keepdims=True)) + 1e-06)

def unit_inverse(lower_part):
    size = lower_part.shape[-1]
    nilpotent = -lower_part
    total = jnp.eye(size, dtype=jnp.float32) + nilpotent
    power = nilpotent
    for level in range(max(1, (size - 1).bit_length()) - 1):
        power = jnp.einsum('nhij,nhjk->nhik', power, power, precision=highest)
        total = total + jnp.einsum('nhij,nhjk->nhik', total, power, precision=highest)
    return total

def block_terms(queries, key_rows, value_rows, beta, gate_log, starts):
    size = queries.shape[2]
    row_ids = lax.broadcasted_iota(jnp.int32, (size, size), 0)
    col_ids = lax.broadcasted_iota(jnp.int32, (size, size), 1)
    gamma = jnp.cumsum(gate_log, axis=-1)
    count = jnp.cumsum(starts, axis=-1)
    linked = (count[:, :, None] == count[:, None, :]) & (row_ids >= col_ids)
    linked = linked[:, None, :, :]
    spread = gamma[..., :, None] - gamma[..., None, :]
    decay = jnp.where(linked, jnp.exp(jnp.where(linked, spread, 0.0)), 0.0)
    head_decay = jnp.where(count == 0.0, 1.0, 0.0)[:, None, :] * jnp.exp(gamma)
    tail_decay = decay[..., size - 1, :]
    key_key = jnp.einsum('nhik,nhjk->nhij', key_rows, key_rows, precision=highest)
    lower_part = jnp.where(row_ids > col_ids, beta[..., :, None] * decay * key_key, 0.0)
    inverse = unit_inverse(lower_part)
    rhs_value = beta[..., None] * value_rows
    rhs_key = (beta * head_decay)[..., None] * key_rows
    u_zero = jnp.einsum('nhij,nhjv->nhiv', inverse, rhs_value, precision=highest)
    z_rows = jnp.einsum('nhij,nhjk->nhik', inverse, rhs_key, precision=highest)
    mixing = decay * jnp.einsum('nhik,nhjk->nhij', queries, key_rows, precision=highest)
    out_zero = jnp.einsum('nhij,nhjv->nhiv', mixing, u_zero, precision=highest)
    carry_q = head_decay[..., None] * queries - jnp.einsum('nhij,nhjk->nhik', mixing, z_rows, precision=highest)
    weighted = tail_decay[..., None] * key_rows
    state_zero = jnp.einsum('nhcv,nhck->nhvk', u_zero, weighted, precision=highest)
    identity = jnp.eye(key_rows.shape[-1], dtype=jnp.float32)
    transfer = head_decay[..., size - 1][..., None, None] * identity - jnp.einsum('nhck,nhcj->nhkj', z_rows, weighted, precision=highest)
    return (out_zero, carry_q, state_zero, transfer)

def run_blocks(out_zero, carry_q, state_zero, transfer, state_in):

    def advance(state, pieces):
        piece_out, piece_q, piece_state, piece_map = pieces
        result = piece_out + jnp.einsum('hck,hvk->hcv', piece_q, state, precision=highest)
        updated = jnp.einsum('hvk,hkj->hvj', state, piece_map, precision=highest) + piece_state
        return (updated, result)
    final, outputs = lax.scan(advance, state_in, (out_zero, carry_q, state_zero, transfer))
    return (outputs, final)

def segment_terms(query_f, key_f, value_f, logits, gate_log, starts):
    token_count, heads = logits.shape
    blocks = token_count // BLOCK

    def split(rows):
        return rows.reshape(blocks, BLOCK, heads, -1).transpose(0, 2, 1, 3)
    beta = jax.nn.sigmoid(logits).reshape(blocks, BLOCK, heads).transpose(0, 2, 1)
    gates = gate_log.reshape(heads, blocks, BLOCK).transpose(1, 0, 2)
    return block_terms(unit_rows(split(query_f)), unit_rows(split(key_f)), split(value_f), beta, gates, starts.reshape(blocks, BLOCK))

def output_from_terms(terms, state_in):
    outputs, final = run_blocks(terms[0], terms[1], terms[2], terms[3], state_in)
    token_count = outputs.shape[0] * outputs.shape[2]
    return (outputs.transpose(0, 2, 1, 3).reshape(token_count, -1), final)

def segment_output(query_f, key_f, value_f, logits, gate_log, starts, state_in):
    return output_from_terms(segment_terms(query_f, key_f, value_f, logits, gate_log, starts), state_in)

def token_plan(row_lengths, positions):
    ends = jnp.cumsum(row_lengths)
    begins = ends - row_lengths
    starts = jnp.any(positions[:, None] == begins[None, :], axis=1).astype(jnp.float32)
    member = ((positions[:, None] >= begins[None, :]) & (positions[:, None] < ends[None, :])).astype(jnp.float32)
    return (starts, member)

def advantages(rewards, prompts):
    same = (prompts[:, None] == prompts[None, :]).astype(jnp.float32)
    return rewards - lax.optimization_barrier(jnp.sum(same * rewards[None, :], axis=1)) / lax.optimization_barrier(jnp.sum(same, axis=1))

def reference(queries, key_rows, value_rows, hidden_in, beta_weight, log_gate, out_grad, lengths, rewards, prompts):
    roll_weight = advantages(rewards, prompts).reshape(N_DP, ROLL) * GROUP_TOKENS / (ROLL * lengths.astype(jnp.float32))
    positions = jnp.arange(GROUP_TOKENS, dtype=jnp.int32)
    starts, member = jax.vmap(token_plan, (0, None))(lengths, positions)
    token_weight = lax.optimization_barrier(jnp.sum(member * roll_weight[:, None, :], axis=-1)).reshape(TOTAL_TOKENS)
    cotangent = out_grad.astype(jnp.float32) * token_weight[:, None]
    logits = jnp.dot(hidden_in, beta_weight, preferred_element_type=jnp.float32)
    width = HALF_HEADS * HEAD_DIM
    zero_state = jnp.zeros((HALF_HEADS, HEAD_DIM, HEAD_DIM), jnp.float32)

    def one_group(pieces):
        query_f, key_f, value_f, group_logits, group_gates, group_starts, group_cot = pieces

        def forward(a_rows, b_rows, c_rows, d_rows, e_rows):
            return segment_output(a_rows, b_rows, c_rows, d_rows, e_rows, group_starts, zero_state)[0]
        primal, backward = jax.vjp(forward, query_f, key_f, value_f, group_logits, group_gates)
        return backward(group_cot)
    grads = lax.map(one_group, (queries.astype(jnp.float32).reshape(N_DP, GROUP_TOKENS, width), key_rows.astype(jnp.float32).reshape(N_DP, GROUP_TOKENS, width), value_rows.astype(jnp.float32).reshape(N_DP, GROUP_TOKENS, width), logits.reshape(N_DP, GROUP_TOKENS, HALF_HEADS), log_gate.reshape(HALF_HEADS, N_DP, GROUP_TOKENS).transpose(1, 0, 2), starts, cotangent.reshape(N_DP, GROUP_TOKENS, width)))
    query_grad = grads[0].reshape(TOTAL_TOKENS, width).astype(jnp.bfloat16)
    key_grad = grads[1].reshape(TOTAL_TOKENS, width).astype(jnp.bfloat16)
    value_grad = grads[2].reshape(TOTAL_TOKENS, width).astype(jnp.bfloat16)
    logit_grad = grads[3].reshape(TOTAL_TOKENS, HALF_HEADS)
    gate_grad = grads[4].transpose(1, 0, 2).reshape(HALF_HEADS, TOTAL_TOKENS)
    beta_weight_grad = jnp.dot(hidden_in.astype(jnp.float32).T, logit_grad, precision=highest, preferred_element_type=jnp.float32)
    return (query_grad, key_grad, value_grad, gate_grad, beta_weight_grad)
```

```python
import functools

import jax
import jax.numpy as jnp
from jax import lax
from jax.experimental import pallas as pl
from jax.experimental.pallas import tpu as pltpu
from jax.sharding import PartitionSpec as P

SMALL = 16
MAP_LAG = 2
GRAD_SLACK = 1
MESH = pl.DeviceIdType.MESH
F32 = jnp.float32
BF16 = jnp.bfloat16


def split(x):
    hi = x.astype(BF16)
    return hi, (x - hi.astype(F32)).astype(BF16)


def left(x):
    return jnp.concatenate(split(x), axis=1)


def left_t(x):
    return jnp.concatenate(split(x), axis=0)


def right(x):
    row = jnp.concatenate(split(x), axis=1)
    return jnp.concatenate([row, row], axis=0)


def right_t(x):
    hi, lo = split(x)
    return jnp.concatenate(
        [jnp.concatenate([hi, hi], axis=1), jnp.concatenate([lo, lo], axis=1)], axis=0
    )


def contract(a, b, dims):
    out = lax.dot_general(a, b, ((dims[:1], dims[1:]), ((), ())), preferred_element_type=F32)
    half = out.shape[1] // 2
    return out[:, :half] + out[:, half:]


def mul(a, b):
    return contract(left(a), right(b), (1, 0))


def mul_t(a, b):
    return contract(left(a), right_t(b), (1, 1))


def t_mul(a, b):
    return contract(left_t(a), right(b), (0, 0))


def stack(*parts):
    return jnp.concatenate(parts, axis=0)


def row_sum(x):
    return jnp.sum(x, axis=1, keepdims=True)


def inverses(lows, rows, cols):
    size = lows[0].shape[0]
    eye = jnp.where(rows == cols, 1.0, 0.0)
    base = min(SMALL, size)
    same = (rows // base) == (cols // base)
    powers = [jnp.where(same, -low, 0.0) for low in lows]
    totals = [eye + power for power in powers]
    powers = [mul(power, power) for power in powers]
    reach = 2
    while reach * 2 < base:
        both = [mul(stack(t, p), p) for t, p in zip(totals, powers)]
        totals = [t + b[:size] for t, b in zip(totals, both)]
        powers = [b[size:] for b in both]
        reach *= 2
    totals = [t + mul(t, p) for t, p in zip(totals, powers)]
    while base < size:
        own = ((rows // (2 * base)) == (cols // (2 * base))) & ((rows // base) != (cols // base))
        parts = [jnp.where(own, low, 0.0) for low in lows]
        mids = [mul(t, part) for t, part in zip(totals, parts)]
        totals = [t - mul(m, t) for t, m in zip(totals, mids)]
        base *= 2
    return totals


def kernel(
    q_ref, k_ref, v_ref, o_ref, cols_ref, rows_ref, hidden_ref,
    dq_ref, dk_ref, dv_ref, dgate_ref, weight_ref,
    inv_ref, mix_ref, dkk_ref, dec_ref, maps_ref, give_ref,
    fpair_ref, bpair_ref, fout_ref, bout_ref, fmate_ref, bmate_ref,
    dlogit_ref, whole_ref, near_out, near_in, far_out, far_in,
    msend, mrecv, fsend, frecv, bsend, brecv, fgive, ftake, bgive, btake,
    nsend, nrecv, wsend, wrecv,
):
    tokens = q_ref.shape[0]
    width = fout_ref.shape[-1]
    turns = fout_ref.shape[0]
    count = lax.axis_size("ctx")
    seg = lax.axis_index("ctx")
    tiers = count // 2
    tier = seg // 2
    side = lax.rem(seg, 2)
    mate = seg + 1 - 2 * side

    barrier = pltpu.get_barrier_semaphore()

    part = lax.axis_index("dp")
    parts = lax.axis_size("dp")
    for by in range(1, count):
        pl.semaphore_signal(
            barrier, inc=1, device_id={"ctx": lax.rem(seg + by, count)}, device_id_type=MESH
        )
    for by in range(1, parts):
        pl.semaphore_signal(
            barrier, inc=1, device_id={"dp": lax.rem(part + by, parts)}, device_id_type=MESH
        )
    pl.semaphore_wait(barrier, count + parts - 2)

    def copy(src, dst, sent, landed, to):
        return pltpu.make_async_remote_copy(
            src_ref=src, dst_ref=dst, send_sem=sent, recv_sem=landed,
            device_id={"ctx": to}, device_id_type=MESH,
        )

    def map_copy(i):
        return copy(give_ref.at[i], maps_ref.at[i, side], msend.at[i], mrecv.at[i], mate)

    def forward_copy(i):
        return copy(fout_ref.at[i], fpair_ref.at[i, 0], fsend.at[i], frecv.at[i], seg + 2)

    def backward_copy(i):
        return copy(bout_ref.at[i], bpair_ref.at[i, 1], bsend.at[i], brecv.at[i], seg - 2)

    def state_copy(i):
        return copy(fpair_ref.at[i, 1 - side], fmate_ref.at[i], fgive.at[i], ftake.at[i], mate)

    def after_copy(i):
        return copy(bpair_ref.at[i, 1 - side], bmate_ref.at[i], bgive.at[i], btake.at[i], mate)

    rows = lax.broadcasted_iota(jnp.int32, (tokens, tokens), 0)
    cols = lax.broadcasted_iota(jnp.int32, (tokens, tokens), 1)
    both_heads = range(2)

    def head_of(turn, j):
        return (side if j == 0 else 1 - side) * turns + turn

    def lanes(h):
        return pl.ds(pl.multiple_of(h * width, width), width)

    def load(ref, h):
        return ref[:, lanes(h)].astype(F32)

    def token_columns(h):
        block = cols_ref[h]
        row_block = rows_ref[h]
        beta, gamma = block[:, 0:1], block[:, 1:2]
        number, weight = block[:, 2:3], block[:, 3:4]
        gamma_row, number_row = row_block[0:1, :], row_block[1:2, :]
        head = jnp.where(number == 0.0, jnp.exp(gamma), 0.0)
        tied = number == number_row[:, tokens - 1:tokens]
        tail = jnp.where(
            tied, jnp.exp(jnp.where(tied, gamma_row[:, tokens - 1:tokens] - gamma, 0.0)), 0.0
        )
        return beta, gamma, number, weight, gamma_row, number_row, head, tail

    def scales(x):
        return lax.rsqrt(row_sum(x * x) + 1e-06)

    def local_part(turn):
        lows, keep = [], []
        for j in both_heads:
            h = head_of(turn, j)
            beta, gamma, number, weight, gamma_row, number_row, head, tail = token_columns(h)
            q, k = load(q_ref, h), load(k_ref, h)
            qh, kh = q * scales(q), k * scales(k)
            linked = (number == number_row) & (rows >= cols)
            decay = jnp.where(linked, jnp.exp(jnp.where(linked, gamma - gamma_row, 0.0)), 0.0)
            both = mul_t(stack(kh, qh), kh)
            dkk = jnp.where(rows > cols, decay * both[:tokens], 0.0)
            mix = decay * both[tokens:]
            dec_ref[turn, j] = decay
            dkk_ref[turn, j] = dkk
            mix_ref[turn, j] = mix
            lows.append(beta * dkk)
            keep.append((h, beta, weight, head, tail, qh, kh, mix))
        invs = inverses(lows, rows, cols)
        for j in both_heads:
            inv_ref[turn, j] = invs[j]
        pairs = []
        for j in both_heads:
            h, beta, weight, head, tail, qh, kh, mix = keep[j]
            v = load(v_ref, h)
            pairs.append(mul(invs[j], jnp.concatenate([beta * v, (beta * head) * kh], axis=1)))
        eye = jnp.where(rows == cols, 1.0, 0.0)
        for j in both_heads:
            h, beta, weight, head, tail, qh, kh, mix = keep[j]
            out = maps_ref.at[turn, side] if j == 0 else give_ref.at[turn]
            z = pairs[j][:, width:]
            ends = t_mul(pairs[j], tail * kh)
            out[0] = head[tokens - 1:tokens, :] * eye - ends[width:]
            out[1] = ends[:width]
            carry = head * qh - mul(mix, z)
            out[2] = t_mul(load(o_ref, h) * weight, carry)

    def forward_step(i):
        @pl.when(tier == 0)
        def _():
            fpair_ref[i, 0] = jnp.zeros((width, width), F32)

        @pl.when(tier > 0)
        def _():
            forward_copy(i).wait_recv()

        second = mul(fpair_ref[i, 0], maps_ref[i, 0, 0]) + maps_ref[i, 0, 1]
        fpair_ref[i, 1] = second

        @pl.when(tier < tiers - 1)
        def _():
            fout_ref[i] = mul(fpair_ref[i, 1], maps_ref[i, 1, 0]) + maps_ref[i, 1, 1]
            forward_copy(i).start()

        state_copy(i).start()

    def backward_step(i):
        @pl.when(tier == tiers - 1)
        def _():
            bpair_ref[i, 1] = jnp.zeros((width, width), F32)

        @pl.when(tier < tiers - 1)
        def _():
            backward_copy(i).wait_recv()

        first = mul_t(bpair_ref[i, 1], maps_ref[i, 1, 0]) + maps_ref[i, 1, 2]
        bpair_ref[i, 0] = first

        @pl.when(tier > 0)
        def _():
            bout_ref[i] = mul_t(bpair_ref[i, 0], maps_ref[i, 0, 0]) + maps_ref[i, 0, 2]
            backward_copy(i).start()

        after_copy(i).start()

    def gradient_part(turn):
        state_copy(turn).wait_recv()
        after_copy(turn).wait_recv()
        upper = jnp.where(rows < cols, 1.0, 0.0).astype(BF16)
        upper = stack(upper, upper)
        keep = []
        afters = [bpair_ref[turn, side], bmate_ref[turn]]
        for j in both_heads:
            h = head_of(turn, j)
            beta, gamma, number, weight, gamma_row, number_row, head, tail = token_columns(h)
            q, k = load(q_ref, h), load(k_ref, h)
            qs, ks = scales(q), scales(k)
            qh, kh = q * qs, k * ks
            state = fpair_ref[turn, side] if j == 0 else fmate_ref[turn]
            both = mul_t(stack(qh, kh), state)
            keep.append((beta, weight, head, tail, qs, ks, qh, kh, state, both[:tokens], both[tokens:]))
        heads = [head_of(turn, j) for j in both_heads]
        rests = [load(v_ref, heads[i]) - keep[i][2] * keep[i][10] for i in both_heads]
        us = [mul(inv_ref[turn, i], keep[i][0] * rests[i]) for i in both_heads]
        dos = [load(o_ref, heads[i]) * keep[i][1] for i in both_heads]
        dus = [
            t_mul(mix_ref[turn, i], dos[i]) + mul_t(keep[i][3] * keep[i][7], afters[i])
            for i in both_heads
        ]
        drs = [t_mul(inv_ref[turn, i], dus[i]) for i in both_heads]
        squares = [mul_t(stack(dos[i], drs[i]), us[i]) for i in both_heads]
        for i in both_heads:
            beta, weight, head, tail, qs, ks, qh, kh, state, qstate, kstate = keep[i]
            h = heads[i]
            u, do, dr, rest, after = us[i], dos[i], drs[i], rests[i], afters[i]
            decay, dkk = dec_ref[turn, i], dkk_ref[turn, i]
            dmix = squares[i][:tokens]
            dlow = jnp.where(rows > cols, -squares[i][tokens:], 0.0)
            inward = mul(stack(head * do, (-beta * head) * dr), state)
            uafter = mul(u, after)
            da = dmix * decay
            dpair = dlow * (beta * decay)
            pairs = stack(da, dpair)
            direct = mul(pairs, kh)
            turned = t_mul(pairs, stack(qh, kh))
            dqh = inward[:tokens] + direct[:tokens]
            dkh = inward[tokens:] + direct[tokens:] + turned + tail * uafter
            dq_ref[:, lanes(h)] = (qs * (dqh - qh * row_sum(qh * dqh))).astype(BF16)
            dk_ref[:, lanes(h)] = (ks * (dkh - kh * row_sum(kh * dkh))).astype(BF16)
            dv_ref[:, lanes(h)] = (beta * dr).astype(BF16)
            lowpart = dlow * dkk
            spread = dmix * mix_ref[turn, i] + beta * lowpart
            across = lax.dot_general(
                left(spread), upper, (((1,), (0,)), ((), ())), preferred_element_type=F32
            )
            total = jnp.sum(row_sum(after * state), axis=0, keepdims=True)
            headgrad = row_sum(do * qstate) - beta * row_sum(dr * kstate)
            headgrad = head * (headgrad + jnp.where(rows[:, :1] == tokens - 1, total, 0.0))
            tailgrad = tail * row_sum(kh * uafter)
            dgate_ref[h] = jnp.sum(
                jnp.where(rows >= cols, across + headgrad, tailgrad), axis=0, keepdims=True
            )
            dbeta = row_sum(dr * rest) + row_sum(lowpart)
            dlogit_ref[h] = dbeta * beta * (1.0 - beta)

    def within(i):
        return (i >= 0) & (i < turns)

    grad_lag = MAP_LAG + tiers + GRAD_SLACK

    def step(t, unused):
        @pl.when(t < turns)
        def _():
            local_part(t)
            map_copy(t).start()

        f = t - MAP_LAG - tier
        b = t - MAP_LAG - (tiers - 1 - tier)
        m = jnp.maximum(f, b)

        @pl.when(within(m))
        def _():
            map_copy(m).wait_recv()

        @pl.when(within(f))
        def _():
            forward_step(f)

        @pl.when(within(b))
        def _():
            backward_step(b)

        @pl.when(within(t - grad_lag))
        def _():
            gradient_part(t - grad_lag)

        return unused

    lax.fori_loop(0, turns + grad_lag, step, 0)

    def drain(i, unused):
        map_copy(i).wait_send()
        state_copy(i).wait_send()
        after_copy(i).wait_send()

        @pl.when(tier < tiers - 1)
        def _():
            forward_copy(i).wait_send()

        @pl.when(tier > 0)
        def _():
            backward_copy(i).wait_send()

        return unused

    logit_grad = jnp.concatenate([dlogit_ref[h] for h in range(2 * turns)], axis=1)
    hidden = hidden_ref[...]
    whole_ref[...] = lax.dot_general(
        left_t(logit_grad), stack(hidden, hidden), (((0,), (0,)), ((), ())),
        preferred_element_type=F32,
    )
    owned = near_out.shape[-1]
    for p in range(parts):
        for c in range(count):
            at = (p * count + c) * owned
            near_out[p, c] = whole_ref[:, at:at + owned]

    def near_copy(by):
        to = lax.rem(part + by, parts)
        return pltpu.make_async_remote_copy(
            src_ref=near_out.at[to], dst_ref=near_in.at[by - 1],
            send_sem=nsend.at[by - 1], recv_sem=nrecv.at[by - 1],
            device_id={"dp": to}, device_id_type=MESH,
        )

    def far_copy(by):
        to = lax.rem(seg + by, count)
        return pltpu.make_async_remote_copy(
            src_ref=far_out.at[to], dst_ref=far_in.at[by - 1],
            send_sem=wsend.at[by - 1], recv_sem=wrecv.at[by - 1],
            device_id={"ctx": to}, device_id_type=MESH,
        )

    for by in range(1, parts):
        near_copy(by).start()
    total = near_out[part]
    for by in range(1, parts):
        near_copy(by).wait_recv()
        total = total + near_in[by - 1]
    far_out[...] = total
    for by in range(1, count):
        far_copy(by).start()
    total = far_out[seg]
    for by in range(1, count):
        far_copy(by).wait_recv()
        total = total + far_in[by - 1]
    weight_ref[...] = total
    for by in range(1, parts):
        near_copy(by).wait_send()
    for by in range(1, count):
        far_copy(by).wait_send()

    lax.fori_loop(0, turns, drain, 0)


def token_plan(row_lengths, positions):
    ends = jnp.cumsum(row_lengths)
    begins = ends - row_lengths
    starts = jnp.any(positions[:, None] == begins[None, :], axis=1).astype(jnp.float32)
    member = (
        (positions[:, None] >= begins[None, :]) & (positions[:, None] < ends[None, :])
    ).astype(jnp.float32)
    return (starts, member)


def advantages(rewards, prompts):
    same = (prompts[:, None] == prompts[None, :]).astype(jnp.float32)
    return rewards - jnp.sum(same * rewards[None, :], axis=1) / jnp.sum(same, axis=1)


def local(
    queries, key_rows, value_rows, hidden_in, beta_weight, log_gate, out_grad,
    lengths, rewards, prompts,
):
    tokens = queries.shape[0]
    heads = beta_weight.shape[1]
    width = queries.shape[1] // heads
    ctx_count = lax.axis_size("ctx")
    roll_count = lengths.shape[1]
    group_tokens = tokens * ctx_count
    positions = lax.axis_index("ctx") * tokens + jnp.arange(tokens, dtype=jnp.int32)
    starts, member = token_plan(lengths[0], positions)
    own_advantage = lax.dynamic_slice_in_dim(
        advantages(rewards, prompts), lax.axis_index("dp") * roll_count, roll_count
    )
    roll_weight = own_advantage * group_tokens / (roll_count * lengths[0].astype(jnp.float32))
    token_weight = jnp.sum(member * roll_weight[None, :], axis=-1)
    logits = jnp.dot(hidden_in, beta_weight, preferred_element_type=jnp.float32)
    beta = jax.nn.sigmoid(logits)
    gamma = jnp.cumsum(log_gate, axis=-1)
    number = jnp.cumsum(starts)
    shared = jnp.broadcast_to(
        jnp.stack([number, token_weight], axis=1)[None], (heads, tokens, 2)
    )
    columns = jnp.concatenate([beta.T[:, :, None], gamma[:, :, None], shared], axis=2)
    lines = jnp.stack([gamma, jnp.broadcast_to(number[None], (heads, tokens))], axis=1)
    turns = heads // 2
    square = (turns, 2, tokens, tokens)
    states = (turns, width, width)
    pairs = (turns, 2, width, width)
    vmem = pl.BlockSpec(memory_space=pltpu.VMEM)
    model = hidden_in.shape[1]
    dp_count = lax.axis_size("dp")
    owned = model // (dp_count * ctx_count)
    dq, dk, dv, dgate, own_grad = pl.pallas_call(
        kernel,
        out_shape=(
            jax.ShapeDtypeStruct(queries.shape, BF16),
            jax.ShapeDtypeStruct(queries.shape, BF16),
            jax.ShapeDtypeStruct(queries.shape, BF16),
            jax.ShapeDtypeStruct((heads, 1, tokens), F32),
            jax.ShapeDtypeStruct((heads, owned), F32),
        ),
        in_specs=[vmem] * 7,
        out_specs=(vmem,) * 5,
        scratch_shapes=[pltpu.VMEM(square, F32)] * 4
        + [
            pltpu.VMEM((turns, 2, 3, width, width), F32),
            pltpu.VMEM((turns, 3, width, width), F32),
        ]
        + [pltpu.VMEM(pairs, F32)] * 2
        + [pltpu.VMEM(states, F32)] * 4
        + [
            pltpu.VMEM((heads, tokens, 1), F32),
            pltpu.VMEM((heads, model), F32),
            pltpu.VMEM((dp_count, ctx_count, heads, owned), F32),
            pltpu.VMEM((dp_count - 1 or 1, ctx_count, heads, owned), F32),
            pltpu.VMEM((ctx_count, heads, owned), F32),
            pltpu.VMEM((ctx_count - 1, heads, owned), F32),
        ]
        + [pltpu.SemaphoreType.DMA((turns,))] * 10
        + [pltpu.SemaphoreType.DMA((dp_count,))] * 2
        + [pltpu.SemaphoreType.DMA((ctx_count,))] * 2,
        compiler_params=pltpu.CompilerParams(
            collective_id=0, has_side_effects=True, vmem_limit_bytes=48 * 2**20
        ),
        name="delta_backward",
    )(queries, key_rows, value_rows, out_grad, columns, lines, hidden_in)
    return (dq, dk, dv, dgate.reshape(heads, tokens), own_grad.T)


def solution(mesh):
    rows = P(("dp", "ctx"), None)
    in_specs = (
        rows, rows, rows, rows, P(), P(None, ("dp", "ctx")), rows, P("dp", None), P(), P(),
    )
    out_specs = (rows, rows, rows, P(None, ("dp", "ctx")), rows)
    return jax.shard_map(local, mesh=mesh, in_specs=in_specs, out_specs=out_specs, check_vma=False)
```

```python
import functools

import jax
import jax.numpy as jnp
from jax import lax
from jax.experimental import pallas as pl
from jax.experimental.pallas import tpu as pltpu
from jax.sharding import PartitionSpec as P

SMALL = 16
MAP_LAG = 2
GRAD_SLACK = 1
MESH = pl.DeviceIdType.MESH
F32 = jnp.float32
BF16 = jnp.bfloat16


def split(x):
    hi = x.astype(BF16)
    return hi, (x - hi.astype(F32)).astype(BF16)


def left(x):
    return jnp.concatenate(split(x), axis=1)


def left_t(x):
    return jnp.concatenate(split(x), axis=0)


def right(x):
    row = jnp.concatenate(split(x), axis=1)
    return jnp.concatenate([row, row], axis=0)


def right_t(x):
    hi, lo = split(x)
    return jnp.concatenate(
        [jnp.concatenate([hi, hi], axis=1), jnp.concatenate([lo, lo], axis=1)], axis=0
    )


def contract(a, b, dims):
    out = lax.dot_general(a, b, ((dims[:1], dims[1:]), ((), ())), preferred_element_type=F32)
    half = out.shape[1] // 2
    return out[:, :half] + out[:, half:]


def mul(a, b):
    return contract(left(a), right(b), (1, 0))


def mul_t(a, b):
    return contract(left(a), right_t(b), (1, 1))


def t_mul(a, b):
    return contract(left_t(a), right(b), (0, 0))


def stack(*parts):
    return jnp.concatenate(parts, axis=0)


def row_sum(x):
    return jnp.sum(x, axis=1, keepdims=True)


def inverses(lows, rows, cols):
    size = lows[0].shape[0]
    eye = jnp.where(rows == cols, 1.0, 0.0)
    base = min(SMALL, size)
    same = (rows // base) == (cols // base)
    powers = [jnp.where(same, -low, 0.0) for low in lows]
    totals = [eye + power for power in powers]
    powers = [mul(power, power) for power in powers]
    reach = 2
    while reach * 2 < base:
        both = [mul(stack(t, p), p) for t, p in zip(totals, powers)]
        totals = [t + b[:size] for t, b in zip(totals, both)]
        powers = [b[size:] for b in both]
        reach *= 2
    totals = [t + mul(t, p) for t, p in zip(totals, powers)]
    while base < size:
        own = ((rows // (2 * base)) == (cols // (2 * base))) & ((rows // base) != (cols // base))
        parts = [jnp.where(own, low, 0.0) for low in lows]
        mids = [mul(t, part) for t, part in zip(totals, parts)]
        totals = [t - mul(m, t) for t, m in zip(totals, mids)]
        base *= 2
    return totals


def kernel(
    length_in, reward_in, prompt_in,
    q_in, k_in, v_in, o_in, hidden_in, proj_in, gate_in,
    dq_ref, dk_ref, dv_ref, dgate_ref, weight_ref,
    length_ref, reward_ref, prompt_ref,
    q_ref, k_ref, v_ref, o_ref, hidden_ref, proj_ref, gate_ref, cols_ref, rows_ref, load_sem,
    inv_ref, mix_ref, dkk_ref, dec_ref, maps_ref, give_ref,
    fpair_ref, bpair_ref, fout_ref, bout_ref, fmate_ref, bmate_ref,
    dlogit_ref, whole_ref, near_out, near_in, far_out, far_in,
    msend, mrecv, fsend, frecv, bsend, brecv, fgive, ftake, bgive, btake,
    nsend, nrecv, wsend, wrecv,
):
    tokens = q_ref.shape[0]
    width = fout_ref.shape[-1]
    turns = fout_ref.shape[0]
    count = lax.axis_size("ctx")
    seg = lax.axis_index("ctx")
    tiers = count // 2
    tier = seg // 2
    side = lax.rem(seg, 2)
    mate = seg + 1 - 2 * side

    loads = [
        pltpu.make_async_copy(src, dst, load_sem.at[n])
        for n, (src, dst) in enumerate([
            (length_in, length_ref), (reward_in, reward_ref), (prompt_in, prompt_ref),
            (gate_in, gate_ref), (proj_in, proj_ref), (hidden_in, hidden_ref), (k_in, k_ref),
            (q_in, q_ref), (v_in, v_ref), (o_in, o_ref),
        ])
    ]
    for load_copy in loads:
        load_copy.start()

    barrier = pltpu.get_barrier_semaphore()

    part = lax.axis_index("dp")
    parts = lax.axis_size("dp")
    for by in range(1, count):
        pl.semaphore_signal(
            barrier, inc=1, device_id={"ctx": lax.rem(seg + by, count)}, device_id_type=MESH
        )
    for by in range(1, parts):
        pl.semaphore_signal(
            barrier, inc=1, device_id={"dp": lax.rem(part + by, parts)}, device_id_type=MESH
        )

    rows = lax.broadcasted_iota(jnp.int32, (tokens, tokens), 0)
    cols = lax.broadcasted_iota(jnp.int32, (tokens, tokens), 1)

    for load_copy in loads[:3]:
        load_copy.wait()
    rolls = length_ref.shape[1]
    amounts = []
    for i in range(rolls):
        own = prompt_ref[part * rolls + i]
        total, members = jnp.zeros((1, tokens), F32), jnp.zeros((1, tokens), F32)
        for j in range(reward_ref.shape[0]):
            same = jnp.where(prompt_ref[j] == own, 1.0, 0.0)
            total = total + same * reward_ref[j]
            members = members + same
        advantage = reward_ref[part * rolls + i] - total / members
        length = jnp.zeros((1, tokens), F32) + length_ref[0, i].astype(F32)
        amounts.append(advantage * (tokens * count) / (rolls * length))

    def plan(spots, spread_out):
        number, weight = jnp.zeros(spots.shape, F32), jnp.zeros(spots.shape, F32)
        begin = 0
        for i in range(rolls):
            end = begin + length_ref[0, i]
            started = (spots >= begin) & (begin >= seg * tokens)
            number = number + jnp.where(started, 1.0, 0.0)
            amount = spread_out(amounts[i])
            weight = weight + jnp.where((spots >= begin) & (spots < end), amount, 0.0)
            begin = end
        return number, weight

    number_row, _ = plan(seg * tokens + cols[:1, :], lambda x: x)
    number_col, weight_col = plan(seg * tokens + rows[:, :1], lambda x: x[:, :1])

    def thirds(x):
        first = x.astype(BF16)
        rest = x - first.astype(F32)
        second = rest.astype(BF16)
        return first, second, (rest - second.astype(F32)).astype(BF16)

    loads[3].wait()
    upto = jnp.where(rows <= cols, 1.0, 0.0).astype(BF16)
    gates = jnp.concatenate(thirds(gate_ref[...]), axis=0)
    heads_all = gate_ref.shape[0]
    sums = lax.dot_general(gates, upto, (((1,), (0,)), ((), ())), preferred_element_type=F32)
    gamma_rows = (sums[2 * heads_all:] + sums[heads_all:2 * heads_all]) + sums[:heads_all]
    for h in range(heads_all):
        rows_ref[h] = jnp.concatenate([gamma_rows[h:h + 1], number_row], axis=0)
    gamma_cols = gamma_rows.T
    loads[4].wait()
    loads[5].wait()
    logits = lax.dot_general(
        hidden_ref[...], proj_ref[...], (((1,), (1,)), ((), ())), preferred_element_type=F32
    )
    betas = jax.nn.sigmoid(logits)
    for h in range(heads_all):
        cols_ref[h] = jnp.concatenate(
            [betas[:, h:h + 1], gamma_cols[:, h:h + 1], number_col, weight_col], axis=1
        )
    for load_copy in loads[6:]:
        load_copy.wait()
    pl.semaphore_wait(barrier, count + parts - 2)

    def copy(src, dst, sent, landed, to):
        return pltpu.make_async_remote_copy(
            src_ref=src, dst_ref=dst, send_sem=sent, recv_sem=landed,
            device_id={"ctx": to}, device_id_type=MESH,
        )

    def map_copy(i):
        return copy(give_ref.at[i], maps_ref.at[i, side], msend.at[i], mrecv.at[i], mate)

    def forward_copy(i):
        return copy(fout_ref.at[i], fpair_ref.at[i, 0], fsend.at[i], frecv.at[i], seg + 2)

    def backward_copy(i):
        return copy(bout_ref.at[i], bpair_ref.at[i, 1], bsend.at[i], brecv.at[i], seg - 2)

    def state_copy(i):
        return copy(fpair_ref.at[i, 1 - side], fmate_ref.at[i], fgive.at[i], ftake.at[i], mate)

    def after_copy(i):
        return copy(bpair_ref.at[i, 1 - side], bmate_ref.at[i], bgive.at[i], btake.at[i], mate)

    both_heads = range(2)

    def head_of(turn, j):
        return (side if j == 0 else 1 - side) * turns + turn

    def lanes(h):
        return pl.ds(pl.multiple_of(h * width, width), width)

    def load(ref, h):
        return ref[:, lanes(h)].astype(F32)

    def token_columns(h):
        block = cols_ref[h]
        row_block = rows_ref[h]
        beta, gamma = block[:, 0:1], block[:, 1:2]
        number, weight = block[:, 2:3], block[:, 3:4]
        gamma_row, number_row = row_block[0:1, :], row_block[1:2, :]
        head = jnp.where(number == 0.0, jnp.exp(gamma), 0.0)
        tied = number == number_row[:, tokens - 1:tokens]
        tail = jnp.where(
            tied, jnp.exp(jnp.where(tied, gamma_row[:, tokens - 1:tokens] - gamma, 0.0)), 0.0
        )
        return beta, gamma, number, weight, gamma_row, number_row, head, tail

    def scales(x):
        return lax.rsqrt(row_sum(x * x) + 1e-06)

    def local_part(turn):
        lows, keep = [], []
        for j in both_heads:
            h = head_of(turn, j)
            beta, gamma, number, weight, gamma_row, number_row, head, tail = token_columns(h)
            q, k = load(q_ref, h), load(k_ref, h)
            qh, kh = q * scales(q), k * scales(k)
            linked = (number == number_row) & (rows >= cols)
            decay = jnp.where(linked, jnp.exp(jnp.where(linked, gamma - gamma_row, 0.0)), 0.0)
            both = mul_t(stack(kh, qh), kh)
            dkk = jnp.where(rows > cols, decay * both[:tokens], 0.0)
            mix = decay * both[tokens:]
            dec_ref[turn, j] = decay
            dkk_ref[turn, j] = dkk
            mix_ref[turn, j] = mix
            lows.append(beta * dkk)
            keep.append((h, beta, weight, head, tail, qh, kh, mix))
        invs = inverses(lows, rows, cols)
        for j in both_heads:
            inv_ref[turn, j] = invs[j]
        pairs = []
        for j in both_heads:
            h, beta, weight, head, tail, qh, kh, mix = keep[j]
            v = load(v_ref, h)
            pairs.append(mul(invs[j], jnp.concatenate([beta * v, (beta * head) * kh], axis=1)))
        eye = jnp.where(rows == cols, 1.0, 0.0)
        for j in both_heads:
            h, beta, weight, head, tail, qh, kh, mix = keep[j]
            out = maps_ref.at[turn, side] if j == 0 else give_ref.at[turn]
            z = pairs[j][:, width:]
            ends = t_mul(pairs[j], tail * kh)
            out[0] = head[tokens - 1:tokens, :] * eye - ends[width:]
            out[1] = ends[:width]
            carry = head * qh - mul(mix, z)
            out[2] = t_mul(load(o_ref, h) * weight, carry)

    def forward_step(i):
        @pl.when(tier == 0)
        def _():
            fpair_ref[i, 0] = jnp.zeros((width, width), F32)

        @pl.when(tier > 0)
        def _():
            forward_copy(i).wait_recv()

        second = mul(fpair_ref[i, 0], maps_ref[i, 0, 0]) + maps_ref[i, 0, 1]
        fpair_ref[i, 1] = second

        @pl.when(tier < tiers - 1)
        def _():
            fout_ref[i] = mul(fpair_ref[i, 1], maps_ref[i, 1, 0]) + maps_ref[i, 1, 1]
            forward_copy(i).start()

        state_copy(i).start()

    def backward_step(i):
        @pl.when(tier == tiers - 1)
        def _():
            bpair_ref[i, 1] = jnp.zeros((width, width), F32)

        @pl.when(tier < tiers - 1)
        def _():
            backward_copy(i).wait_recv()

        first = mul_t(bpair_ref[i, 1], maps_ref[i, 1, 0]) + maps_ref[i, 1, 2]
        bpair_ref[i, 0] = first

        @pl.when(tier > 0)
        def _():
            bout_ref[i] = mul_t(bpair_ref[i, 0], maps_ref[i, 0, 0]) + maps_ref[i, 0, 2]
            backward_copy(i).start()

        after_copy(i).start()

    def gradient_part(turn):
        state_copy(turn).wait_recv()
        after_copy(turn).wait_recv()
        upper = jnp.where(rows < cols, 1.0, 0.0).astype(BF16)
        upper = stack(upper, upper)
        keep = []
        afters = [bpair_ref[turn, side], bmate_ref[turn]]
        for j in both_heads:
            h = head_of(turn, j)
            beta, gamma, number, weight, gamma_row, number_row, head, tail = token_columns(h)
            q, k = load(q_ref, h), load(k_ref, h)
            qs, ks = scales(q), scales(k)
            qh, kh = q * qs, k * ks
            state = fpair_ref[turn, side] if j == 0 else fmate_ref[turn]
            both = mul_t(stack(qh, kh), state)
            keep.append((beta, weight, head, tail, qs, ks, qh, kh, state, both[:tokens], both[tokens:]))
        heads = [head_of(turn, j) for j in both_heads]
        rests = [load(v_ref, heads[i]) - keep[i][2] * keep[i][10] for i in both_heads]
        us = [mul(inv_ref[turn, i], keep[i][0] * rests[i]) for i in both_heads]
        dos = [load(o_ref, heads[i]) * keep[i][1] for i in both_heads]
        dus = [
            t_mul(mix_ref[turn, i], dos[i]) + mul_t(keep[i][3] * keep[i][7], afters[i])
            for i in both_heads
        ]
        drs = [t_mul(inv_ref[turn, i], dus[i]) for i in both_heads]
        squares = [mul_t(stack(dos[i], drs[i]), us[i]) for i in both_heads]
        for i in both_heads:
            beta, weight, head, tail, qs, ks, qh, kh, state, qstate, kstate = keep[i]
            h = heads[i]
            u, do, dr, rest, after = us[i], dos[i], drs[i], rests[i], afters[i]
            decay, dkk = dec_ref[turn, i], dkk_ref[turn, i]
            dmix = squares[i][:tokens]
            dlow = jnp.where(rows > cols, -squares[i][tokens:], 0.0)
            inward = mul(stack(head * do, (-beta * head) * dr), state)
            uafter = mul(u, after)
            da = dmix * decay
            dpair = dlow * (beta * decay)
            pairs = stack(da, dpair)
            direct = mul(pairs, kh)
            turned = t_mul(pairs, stack(qh, kh))
            dqh = inward[:tokens] + direct[:tokens]
            dkh = inward[tokens:] + direct[tokens:] + turned + tail * uafter
            dq_ref[:, lanes(h)] = (qs * (dqh - qh * row_sum(qh * dqh))).astype(BF16)
            dk_ref[:, lanes(h)] = (ks * (dkh - kh * row_sum(kh * dkh))).astype(BF16)
            dv_ref[:, lanes(h)] = (beta * dr).astype(BF16)
            lowpart = dlow * dkk
            spread = dmix * mix_ref[turn, i] + beta * lowpart
            across = lax.dot_general(
                left(spread), upper, (((1,), (0,)), ((), ())), preferred_element_type=F32
            )
            total = jnp.sum(row_sum(after * state), axis=0, keepdims=True)
            headgrad = row_sum(do * qstate) - beta * row_sum(dr * kstate)
            headgrad = head * (headgrad + jnp.where(rows[:, :1] == tokens - 1, total, 0.0))
            tailgrad = tail * row_sum(kh * uafter)
            dgate_ref[pl.ds(h, 1), :] = jnp.sum(
                jnp.where(rows >= cols, across + headgrad, tailgrad), axis=0, keepdims=True
            )
            dbeta = row_sum(dr * rest) + row_sum(lowpart)
            dlogit_ref[h] = dbeta * beta * (1.0 - beta)

    def within(i):
        return (i >= 0) & (i < turns)

    grad_lag = MAP_LAG + tiers + GRAD_SLACK

    def step(t, unused):
        @pl.when(t < turns)
        def _():
            local_part(t)
            map_copy(t).start()

        f = t - MAP_LAG - tier
        b = t - MAP_LAG - (tiers - 1 - tier)
        m = jnp.maximum(f, b)

        @pl.when(within(m))
        def _():
            map_copy(m).wait_recv()

        @pl.when(within(f))
        def _():
            forward_step(f)

        @pl.when(within(b))
        def _():
            backward_step(b)

        @pl.when(within(t - grad_lag))
        def _():
            gradient_part(t - grad_lag)

        return unused

    lax.fori_loop(0, turns + grad_lag, step, 0)

    def drain(i, unused):
        map_copy(i).wait_send()
        state_copy(i).wait_send()
        after_copy(i).wait_send()

        @pl.when(tier < tiers - 1)
        def _():
            forward_copy(i).wait_send()

        @pl.when(tier > 0)
        def _():
            backward_copy(i).wait_send()

        return unused

    logit_grad = jnp.concatenate([dlogit_ref[h] for h in range(2 * turns)], axis=1)
    hidden = hidden_ref[...]
    whole_ref[...] = lax.dot_general(
        left_t(logit_grad), stack(hidden, hidden), (((0,), (0,)), ((), ())),
        preferred_element_type=F32,
    )
    owned = near_out.shape[-1]
    for p in range(parts):
        for c in range(count):
            at = (p * count + c) * owned
            near_out[p, c] = whole_ref[:, at:at + owned]

    def near_copy(by):
        to = lax.rem(part + by, parts)
        return pltpu.make_async_remote_copy(
            src_ref=near_out.at[to], dst_ref=near_in.at[by - 1],
            send_sem=nsend.at[by - 1], recv_sem=nrecv.at[by - 1],
            device_id={"dp": to}, device_id_type=MESH,
        )

    def far_copy(by):
        to = lax.rem(seg + by, count)
        return pltpu.make_async_remote_copy(
            src_ref=far_out.at[to], dst_ref=far_in.at[by - 1],
            send_sem=wsend.at[by - 1], recv_sem=wrecv.at[by - 1],
            device_id={"ctx": to}, device_id_type=MESH,
        )

    for by in range(1, parts):
        near_copy(by).start()
    total = near_out[part]
    for by in range(1, parts):
        near_copy(by).wait_recv()
        total = total + near_in[by - 1]
    far_out[...] = total
    for by in range(1, count):
        far_copy(by).start()
    total = far_out[seg]
    for by in range(1, count):
        far_copy(by).wait_recv()
        total = total + far_in[by - 1]
    weight_ref[...] = total
    for by in range(1, parts):
        near_copy(by).wait_send()
    for by in range(1, count):
        far_copy(by).wait_send()

    lax.fori_loop(0, turns, drain, 0)


def move_kernel(*refs):
    half = len(refs) // 2
    sems = refs[-1]
    copies = [pltpu.make_async_copy(refs[n], refs[half + n], sems.at[n]) for n in range(half)]
    for move in copies:
        move.start()
    for move in copies:
        move.wait()


def local(
    queries, key_rows, value_rows, hidden_in, beta_weight, log_gate, out_grad,
    lengths, rewards, prompts,
):
    tokens = queries.shape[0]
    heads = beta_weight.shape[1]
    width = queries.shape[1] // heads
    ctx_count = lax.axis_size("ctx")
    turns = heads // 2
    square = (turns, 2, tokens, tokens)
    states = (turns, width, width)
    pairs = (turns, 2, width, width)
    vmem = pl.BlockSpec(memory_space=pltpu.VMEM)
    hbm = pl.BlockSpec(memory_space=pltpu.HBM)
    model = hidden_in.shape[1]
    dp_count = lax.axis_size("dp")
    owned = model // (dp_count * ctx_count)
    out_shape = (
        jax.ShapeDtypeStruct(queries.shape, BF16),
        jax.ShapeDtypeStruct(queries.shape, BF16),
        jax.ShapeDtypeStruct(queries.shape, BF16),
        jax.ShapeDtypeStruct((heads, tokens), F32),
        jax.ShapeDtypeStruct((heads, owned), F32),
    )
    grads = pl.pallas_call(
        kernel,
        out_shape=out_shape,
        in_specs=[hbm] * 10,
        out_specs=(vmem,) * 5,
        scratch_shapes=[
            pltpu.SMEM(lengths.shape, jnp.int32),
            pltpu.SMEM(rewards.shape, F32),
            pltpu.SMEM(prompts.shape, jnp.int32),
        ]
        + [pltpu.VMEM(queries.shape, BF16)] * 4
        + [
            pltpu.VMEM(hidden_in.shape, BF16),
            pltpu.VMEM((heads, model), BF16),
            pltpu.VMEM(log_gate.shape, F32),
            pltpu.VMEM((heads, tokens, 4), F32),
            pltpu.VMEM((heads, 2, tokens), F32),
            pltpu.SemaphoreType.DMA((10,)),
        ]
        + [pltpu.VMEM(square, F32)] * 4
        + [
            pltpu.VMEM((turns, 2, 3, width, width), F32),
            pltpu.VMEM((turns, 3, width, width), F32),
        ]
        + [pltpu.VMEM(pairs, F32)] * 2
        + [pltpu.VMEM(states, F32)] * 4
        + [
            pltpu.VMEM((heads, tokens, 1), F32),
            pltpu.VMEM((heads, model), F32),
            pltpu.VMEM((dp_count, ctx_count, heads, owned), F32),
            pltpu.VMEM((dp_count - 1 or 1, ctx_count, heads, owned), F32),
            pltpu.VMEM((ctx_count, heads, owned), F32),
            pltpu.VMEM((ctx_count - 1, heads, owned), F32),
        ]
        + [pltpu.SemaphoreType.DMA((turns,))] * 10
        + [pltpu.SemaphoreType.DMA((dp_count,))] * 2
        + [pltpu.SemaphoreType.DMA((ctx_count,))] * 2,
        compiler_params=pltpu.CompilerParams(
            collective_id=0, has_side_effects=True, vmem_limit_bytes=48 * 2**20
        ),
        name="delta_backward",
    )(
        *[pltpu.with_memory_space_constraint(x, pltpu.HBM) for x in (
            lengths, rewards, prompts,
            queries, key_rows, value_rows, out_grad, hidden_in, beta_weight.T, log_gate,
        )],
    )
    dq, dk, dv, dgate, own_grad = pl.pallas_call(
        move_kernel,
        out_shape=out_shape,
        in_specs=[vmem] * 5,
        out_specs=(hbm,) * 5,
        scratch_shapes=[pltpu.SemaphoreType.DMA((5,))],
        compiler_params=pltpu.CompilerParams(vmem_limit_bytes=4 * 2**20),
        name="store_grads",
    )(*grads)
    return (dq, dk, dv, dgate, own_grad.T)


def solution(mesh):
    rows = P(("dp", "ctx"), None)
    in_specs = (
        rows, rows, rows, rows, P(), P(None, ("dp", "ctx")), rows, P("dp", None), P(), P(),
    )
    out_specs = (rows, rows, rows, P(None, ("dp", "ctx")), rows)
    return jax.shard_map(local, mesh=mesh, in_specs=in_specs, out_specs=out_specs, check_vma=False)
```

```python
import functools

import jax
import jax.numpy as jnp
from jax import lax
from jax.experimental import pallas as pl
from jax.experimental.pallas import tpu as pltpu
from jax.sharding import PartitionSpec as P

SMALL = 16
MAP_LAG = 2
GRAD_SLACK = 1
DETOUR_LAG = 2
MANY = (1, 3, 5)
FEW = (3,)
EXTRA = (4,)
MESH = pl.DeviceIdType.MESH
F32 = jnp.float32
BF16 = jnp.bfloat16


def split(x):
    hi = x.astype(BF16)
    return hi, (x - hi.astype(F32)).astype(BF16)


def left(x):
    return jnp.concatenate(split(x), axis=1)


def left_t(x):
    return jnp.concatenate(split(x), axis=0)


def right(x):
    row = jnp.concatenate(split(x), axis=1)
    return jnp.concatenate([row, row], axis=0)


def right_t(x):
    hi, lo = split(x)
    return jnp.concatenate(
        [jnp.concatenate([hi, hi], axis=1), jnp.concatenate([lo, lo], axis=1)], axis=0
    )


def contract(a, b, dims):
    out = lax.dot_general(a, b, ((dims[:1], dims[1:]), ((), ())), preferred_element_type=F32)
    half = out.shape[1] // 2
    return out[:, :half] + out[:, half:]


def mul(a, b):
    return contract(left(a), right(b), (1, 0))


def mul_t(a, b):
    return contract(left(a), right_t(b), (1, 1))


def t_mul(a, b):
    return contract(left_t(a), right(b), (0, 0))


def stack(*parts):
    return jnp.concatenate(parts, axis=0)


def row_sum(x):
    return jnp.sum(x, axis=1, keepdims=True)


def inverses(lows, rows, cols):
    size = lows[0].shape[0]
    eye = jnp.where(rows == cols, 1.0, 0.0)
    base = min(SMALL, size)
    same = (rows // base) == (cols // base)
    powers = [jnp.where(same, -low, 0.0) for low in lows]
    totals = [eye + power for power in powers]
    powers = [mul(power, power) for power in powers]
    reach = 2
    while reach * 2 < base:
        both = [mul(stack(t, p), p) for t, p in zip(totals, powers)]
        totals = [t + b[:size] for t, b in zip(totals, both)]
        powers = [b[size:] for b in both]
        reach *= 2
    totals = [t + mul(t, p) for t, p in zip(totals, powers)]
    while base < size:
        own = ((rows // (2 * base)) == (cols // (2 * base))) & ((rows // base) != (cols // base))
        parts = [jnp.where(own, low, 0.0) for low in lows]
        mids = [mul(t, part) for t, part in zip(totals, parts)]
        totals = [t - mul(m, t) for t, m in zip(totals, mids)]
        base *= 2
    return totals


def kernel(
    length_in, reward_in, prompt_in,
    q_in, k_in, v_in, o_in, hidden_in, proj_in, gate_in,
    dq_ref, dk_ref, dv_ref, dgate_ref, weight_ref,
    length_ref, reward_ref, prompt_ref,
    q_ref, k_ref, v_ref, o_ref, hidden_ref, proj_ref, gate_ref, cols_ref, rows_ref, load_sem,
    inv_ref, mix_ref, dkk_ref, dec_ref, maps_ref, give_ref,
    detour_ref, fpair_ref, bpair_ref, fout_ref, bout_ref, fmate_ref, bmate_ref,
    dlogit_ref,
    msend, mrecv, fsend, frecv, bsend, brecv, fgive, ftake, bgive, btake,
    dsend, drecv, *sums,
):
    early, late = sums[:len(sums) // 2], sums[len(sums) // 2:]
    tokens = q_ref.shape[0]
    width = fout_ref.shape[-1]
    turns = fout_ref.shape[0]
    count = lax.axis_size("ctx")
    seg = lax.axis_index("ctx")
    tiers = count // 2
    tier = seg // 2
    side = lax.rem(seg, 2)
    mate = seg + 1 - 2 * side

    loads = [
        pltpu.make_async_copy(src, dst, load_sem.at[n])
        for n, (src, dst) in enumerate([
            (length_in, length_ref), (reward_in, reward_ref), (prompt_in, prompt_ref),
            (gate_in, gate_ref), (proj_in, proj_ref), (hidden_in, hidden_ref), (k_in, k_ref),
            (q_in, q_ref), (v_in, v_ref), (o_in, o_ref),
        ])
    ]
    for load_copy in loads:
        load_copy.start()

    barrier = pltpu.get_barrier_semaphore()

    part = lax.axis_index("dp")
    parts = lax.axis_size("dp")
    for by in range(1, count):
        pl.semaphore_signal(
            barrier, inc=1, device_id={"ctx": lax.rem(seg + by, count)}, device_id_type=MESH
        )
    for by in range(1, parts):
        pl.semaphore_signal(
            barrier, inc=1, device_id={"dp": lax.rem(part + by, parts)}, device_id_type=MESH
        )

    rows = lax.broadcasted_iota(jnp.int32, (tokens, tokens), 0)
    cols = lax.broadcasted_iota(jnp.int32, (tokens, tokens), 1)

    for load_copy in loads[:3]:
        load_copy.wait()
    rolls = length_ref.shape[1]
    amounts = []
    for i in range(rolls):
        own = prompt_ref[part * rolls + i]
        total, members = jnp.zeros((1, tokens), F32), jnp.zeros((1, tokens), F32)
        for j in range(reward_ref.shape[0]):
            same = jnp.where(prompt_ref[j] == own, 1.0, 0.0)
            total = total + same * reward_ref[j]
            members = members + same
        advantage = reward_ref[part * rolls + i] - total / members
        length = jnp.zeros((1, tokens), F32) + length_ref[0, i].astype(F32)
        amounts.append(advantage * (tokens * count) / (rolls * length))

    def plan(spots, spread_out):
        number, weight = jnp.zeros(spots.shape, F32), jnp.zeros(spots.shape, F32)
        begin = 0
        for i in range(rolls):
            end = begin + length_ref[0, i]
            started = (spots >= begin) & (begin >= seg * tokens)
            number = number + jnp.where(started, 1.0, 0.0)
            amount = spread_out(amounts[i])
            weight = weight + jnp.where((spots >= begin) & (spots < end), amount, 0.0)
            begin = end
        return number, weight

    number_row, _ = plan(seg * tokens + cols[:1, :], lambda x: x)
    number_col, weight_col = plan(seg * tokens + rows[:, :1], lambda x: x[:, :1])

    def thirds(x):
        first = x.astype(BF16)
        rest = x - first.astype(F32)
        second = rest.astype(BF16)
        return first, second, (rest - second.astype(F32)).astype(BF16)

    loads[3].wait()
    upto = jnp.where(rows <= cols, 1.0, 0.0).astype(BF16)
    gates = jnp.concatenate(thirds(gate_ref[...]), axis=0)
    heads_all = gate_ref.shape[0]
    sums = lax.dot_general(gates, upto, (((1,), (0,)), ((), ())), preferred_element_type=F32)
    gamma_rows = (sums[2 * heads_all:] + sums[heads_all:2 * heads_all]) + sums[:heads_all]
    for h in range(heads_all):
        rows_ref[h] = jnp.concatenate([gamma_rows[h:h + 1], number_row], axis=0)
    gamma_cols = gamma_rows.T
    loads[4].wait()
    loads[5].wait()
    logits = lax.dot_general(
        hidden_ref[...], proj_ref[...], (((1,), (1,)), ((), ())), preferred_element_type=F32
    )
    betas = jax.nn.sigmoid(logits)
    for h in range(heads_all):
        cols_ref[h] = jnp.concatenate(
            [betas[:, h:h + 1], gamma_cols[:, h:h + 1], number_col, weight_col], axis=1
        )
    for load_copy in loads[6:]:
        load_copy.wait()
    pl.semaphore_wait(barrier, count + parts - 2)

    def copy(src, dst, sent, landed, to):
        return pltpu.make_async_remote_copy(
            src_ref=src, dst_ref=dst, send_sem=sent, recv_sem=landed,
            device_id={"ctx": to}, device_id_type=MESH,
        )

    first_tier, last_tier = tier == 0, tier == tiers - 1
    low, high = side == 0, side == 1
    sends_one = (first_tier & low) | (last_tier & high)
    takes_one = (first_tier & high) | (last_tier & low)

    def among(i, some):
        return functools.reduce(jnp.logical_or, [i == n for n in some])

    lower_mid, upper_mid = tier == 1, tier == tiers - 2

    def goes_down(i):
        edge = lower_mid & ((low & among(i, MANY)) | (high & among(i, FEW)))
        return (tiers >= 4) & (edge | (upper_mid & low & among(i, EXTRA)))

    def goes_up(i):
        edge = upper_mid & ((high & among(i, MANY)) | (low & among(i, FEW)))
        return (tiers >= 4) & (edge | (lower_mid & high & among(i, EXTRA)))

    def passes_up(i):
        edge = first_tier & ((high & among(i, MANY)) | (low & among(i, FEW)))
        return (tiers >= 4) & (edge | ((tier == tiers - 3) & high & among(i, EXTRA)))

    def passes_down(i):
        edge = last_tier & ((low & among(i, MANY)) | (high & among(i, FEW)))
        return (tiers >= 4) & (edge | ((tier == 2) & low & among(i, EXTRA)))

    def map_copy(i):
        return copy(give_ref.at[i], maps_ref.at[i, side], msend.at[i], mrecv.at[i], mate)

    def one_copy(i):
        return copy(
            give_ref.at[i, 1 + side], maps_ref.at[i, side, 1 + side], msend.at[i], mrecv.at[i],
            mate,
        )

    def detour_copy(i):
        via = mate + jnp.where(goes_down(i), -2, 2)
        return copy(give_ref.at[i], detour_ref.at[i], msend.at[i], drecv.at[i], via)

    def pass_copy(i):
        to = seg + jnp.where(passes_up(i), 2, -2)
        return copy(detour_ref.at[i], maps_ref.at[i, 1 - side], dsend.at[i], mrecv.at[i], to)

    def forward_copy(i):
        return copy(fout_ref.at[i], fpair_ref.at[i, 0], fsend.at[i], frecv.at[i], seg + 2)

    def backward_copy(i):
        return copy(bout_ref.at[i], bpair_ref.at[i, 1], bsend.at[i], brecv.at[i], seg - 2)

    def state_copy(i):
        return copy(fpair_ref.at[i, 1 - side], fmate_ref.at[i], fgive.at[i], ftake.at[i], mate)

    def after_copy(i):
        return copy(bpair_ref.at[i, 1 - side], bmate_ref.at[i], bgive.at[i], btake.at[i], mate)

    both_heads = range(2)

    def head_of(turn, j):
        return (side if j == 0 else 1 - side) * turns + turn

    def lanes(h):
        return pl.ds(pl.multiple_of(h * width, width), width)

    def load(ref, h):
        return ref[:, lanes(h)].astype(F32)

    def token_columns(h):
        block = cols_ref[h]
        row_block = rows_ref[h]
        beta, gamma = block[:, 0:1], block[:, 1:2]
        number, weight = block[:, 2:3], block[:, 3:4]
        gamma_row, number_row = row_block[0:1, :], row_block[1:2, :]
        head = jnp.where(number == 0.0, jnp.exp(gamma), 0.0)
        tied = number == number_row[:, tokens - 1:tokens]
        tail = jnp.where(
            tied, jnp.exp(jnp.where(tied, gamma_row[:, tokens - 1:tokens] - gamma, 0.0)), 0.0
        )
        return beta, gamma, number, weight, gamma_row, number_row, head, tail

    def scales(x):
        return lax.rsqrt(row_sum(x * x) + 1e-06)

    def local_part(turn):
        lows, keep = [], []
        for j in both_heads:
            h = head_of(turn, j)
            beta, gamma, number, weight, gamma_row, number_row, head, tail = token_columns(h)
            q, k = load(q_ref, h), load(k_ref, h)
            qh, kh = q * scales(q), k * scales(k)
            linked = (number == number_row) & (rows >= cols)
            decay = jnp.where(linked, jnp.exp(jnp.where(linked, gamma - gamma_row, 0.0)), 0.0)
            both = mul_t(stack(kh, qh), kh)
            dkk = jnp.where(rows > cols, decay * both[:tokens], 0.0)
            mix = decay * both[tokens:]
            dec_ref[turn, j] = decay
            dkk_ref[turn, j] = dkk
            mix_ref[turn, j] = mix
            lows.append(beta * dkk)
            keep.append((h, beta, weight, head, tail, qh, kh, mix))
        invs = inverses(lows, rows, cols)
        for j in both_heads:
            inv_ref[turn, j] = invs[j]
        pairs = []
        for j in both_heads:
            h, beta, weight, head, tail, qh, kh, mix = keep[j]
            v = load(v_ref, h)
            pairs.append(mul(invs[j], jnp.concatenate([beta * v, (beta * head) * kh], axis=1)))
        eye = jnp.where(rows == cols, 1.0, 0.0)
        for j in both_heads:
            h, beta, weight, head, tail, qh, kh, mix = keep[j]
            out = maps_ref.at[turn, side] if j == 0 else give_ref.at[turn]
            z = pairs[j][:, width:]
            ends = t_mul(pairs[j], tail * kh)
            out[0] = head[tokens - 1:tokens, :] * eye - ends[width:]
            out[1] = ends[:width]
            carry = head * qh - mul(mix, z)
            out[2] = t_mul(load(o_ref, h) * weight, carry)

    def forward_step(i):
        @pl.when(first_tier)
        def _():
            fpair_ref[i, 0] = jnp.zeros((width, width), F32)
            fpair_ref[i, 1] = maps_ref[i, 0, 1]

        @pl.when(jnp.logical_not(first_tier))
        def _():
            forward_copy(i).wait_recv()
            fpair_ref[i, 1] = mul(fpair_ref[i, 0], maps_ref[i, 0, 0]) + maps_ref[i, 0, 1]

        @pl.when(jnp.logical_not(last_tier))
        def _():
            fout_ref[i] = mul(fpair_ref[i, 1], maps_ref[i, 1, 0]) + maps_ref[i, 1, 1]
            forward_copy(i).start()

        @pl.when(jnp.logical_not(first_tier & high))
        def _():
            state_copy(i).start()

    def backward_step(i):
        @pl.when(last_tier)
        def _():
            bpair_ref[i, 1] = jnp.zeros((width, width), F32)
            bpair_ref[i, 0] = maps_ref[i, 1, 2]

        @pl.when(jnp.logical_not(last_tier))
        def _():
            backward_copy(i).wait_recv()
            bpair_ref[i, 0] = mul_t(bpair_ref[i, 1], maps_ref[i, 1, 0]) + maps_ref[i, 1, 2]

        @pl.when(jnp.logical_not(first_tier))
        def _():
            bout_ref[i] = mul_t(bpair_ref[i, 0], maps_ref[i, 0, 0]) + maps_ref[i, 0, 2]
            backward_copy(i).start()

        @pl.when(jnp.logical_not(last_tier & low))
        def _():
            after_copy(i).start()

    def gradient_first(turn):
        @pl.when(first_tier & low)
        def _():
            fmate_ref[turn] = jnp.zeros((width, width), F32)

        @pl.when(jnp.logical_not(first_tier & low))
        def _():
            state_copy(turn).wait_recv()

        @pl.when(last_tier & high)
        def _():
            bmate_ref[turn] = jnp.zeros((width, width), F32)

        @pl.when(jnp.logical_not(last_tier & high))
        def _():
            after_copy(turn).wait_recv()

        upper = jnp.where(rows < cols, 1.0, 0.0).astype(BF16)
        upper = stack(upper, upper)
        keep = []
        afters = [bpair_ref[turn, side], bmate_ref[turn]]
        for j in both_heads:
            h = head_of(turn, j)
            beta, gamma, number, weight, gamma_row, number_row, head, tail = token_columns(h)
            q, k = load(q_ref, h), load(k_ref, h)
            qs, ks = scales(q), scales(k)
            qh, kh = q * qs, k * ks
            state = fpair_ref[turn, side] if j == 0 else fmate_ref[turn]
            both = mul_t(stack(qh, kh), state)
            keep.append((beta, weight, head, tail, qs, ks, qh, kh, state, both[:tokens], both[tokens:]))
        heads = [head_of(turn, j) for j in both_heads]
        rests = [load(v_ref, heads[i]) - keep[i][2] * keep[i][10] for i in both_heads]
        us = [mul(inv_ref[turn, i], keep[i][0] * rests[i]) for i in both_heads]
        dos = [load(o_ref, heads[i]) * keep[i][1] for i in both_heads]
        dus = [
            t_mul(mix_ref[turn, i], dos[i]) + mul_t(keep[i][3] * keep[i][7], afters[i])
            for i in both_heads
        ]
        drs = [t_mul(inv_ref[turn, i], dus[i]) for i in both_heads]
        squares = [mul_t(stack(dos[i], drs[i]), us[i]) for i in both_heads]
        lows = []
        for i in both_heads:
            beta = keep[i][0]
            dlow = jnp.where(rows > cols, -squares[i][tokens:], 0.0)
            lowpart = dlow * dkk_ref[turn, i]
            dbeta = row_sum(drs[i] * rests[i]) + row_sum(lowpart)
            dlogit_ref[heads[i]] = dbeta * beta * (1.0 - beta)
            lows.append((dlow, lowpart))
        return upper, keep, afters, heads, us, dos, drs, squares, lows

    def gradient_rest(turn, values):
        upper, keep, afters, heads, us, dos, drs, squares, lows = values
        for i in both_heads:
            beta, weight, head, tail, qs, ks, qh, kh, state, qstate, kstate = keep[i]
            h = heads[i]
            u, do, dr, after = us[i], dos[i], drs[i], afters[i]
            decay = dec_ref[turn, i]
            dlow, lowpart = lows[i]
            dmix = squares[i][:tokens]
            inward = mul(stack(head * do, (-beta * head) * dr), state)
            uafter = mul(u, after)
            da = dmix * decay
            dpair = dlow * (beta * decay)
            pairs = stack(da, dpair)
            direct = mul(pairs, kh)
            turned = t_mul(pairs, stack(qh, kh))
            dqh = inward[:tokens] + direct[:tokens]
            dkh = inward[tokens:] + direct[tokens:] + turned + tail * uafter
            dq_ref[:, lanes(h)] = (qs * (dqh - qh * row_sum(qh * dqh))).astype(BF16)
            dk_ref[:, lanes(h)] = (ks * (dkh - kh * row_sum(kh * dkh))).astype(BF16)
            dv_ref[:, lanes(h)] = (beta * dr).astype(BF16)
            spread = dmix * mix_ref[turn, i] + beta * lowpart
            across = lax.dot_general(
                left(spread), upper, (((1,), (0,)), ((), ())), preferred_element_type=F32
            )
            total = jnp.sum(row_sum(after * state), axis=0, keepdims=True)
            headgrad = row_sum(do * qstate) - beta * row_sum(dr * kstate)
            headgrad = head * (headgrad + jnp.where(rows[:, :1] == tokens - 1, total, 0.0))
            tailgrad = tail * row_sum(kh * uafter)
            dgate_ref[pl.ds(h, 1), :] = jnp.sum(
                jnp.where(rows >= cols, across + headgrad, tailgrad), axis=0, keepdims=True
            )

    def within(i):
        return (i >= 0) & (i < turns)

    grad_lag = MAP_LAG + tiers + GRAD_SLACK

    def step(t, unused):
        @pl.when(t < turns)
        def _():
            local_part(t)
            detour = goes_down(t) | goes_up(t)

            @pl.when(sends_one)
            def _():
                one_copy(t).start()

            @pl.when(detour)
            def _():
                detour_copy(t).start()

            @pl.when(jnp.logical_not(sends_one | detour))
            def _():
                map_copy(t).start()

        d = t - DETOUR_LAG

        @pl.when(within(d) & (passes_up(d) | passes_down(d)))
        def _():
            detour_copy(d).wait_recv()
            pass_copy(d).start()

        f = t - MAP_LAG - tier
        b = t - MAP_LAG - (tiers - 1 - tier)
        m = jnp.maximum(f, b)

        @pl.when(within(m))
        def _():
            @pl.when(takes_one)
            def _():
                one_copy(m).wait_recv()

            @pl.when(jnp.logical_not(takes_one))
            def _():
                map_copy(m).wait_recv()

        @pl.when(within(f))
        def _():
            forward_step(f)

        @pl.when(within(b))
        def _():
            backward_step(b)

        @pl.when(within(t - grad_lag))
        def _():
            g = t - grad_lag

            @pl.when(g == cut)
            def _():
                early_begin()

            values = gradient_first(g)

            @pl.when(g == turns - 1)
            def _():
                late_begin()

            gradient_rest(g, values)

            @pl.when(g == cut)
            def _():
                early_middle()

        return unused


    def drain(i, unused):
        @pl.when(sends_one)
        def _():
            one_copy(i).wait_send()

        @pl.when(jnp.logical_not(sends_one))
        def _():
            map_copy(i).wait_send()

        @pl.when(passes_up(i) | passes_down(i))
        def _():
            pass_copy(i).wait_send()

        @pl.when(jnp.logical_not(first_tier & high))
        def _():
            state_copy(i).wait_send()

        @pl.when(jnp.logical_not(last_tier & low))
        def _():
            after_copy(i).wait_send()

        @pl.when(jnp.logical_not(last_tier))
        def _():
            forward_copy(i).wait_send()

        @pl.when(jnp.logical_not(first_tier))
        def _():
            backward_copy(i).wait_send()

        return unused

    hidden = hidden_ref[...]
    hidden = stack(hidden, hidden)

    def reduction(some, whole_ref, near_out, near_in, far_out, far_in, nsend, nrecv, wsend, wrecv):
        owned = weight_ref.shape[1]
        breadth = near_out.shape[-1]
        model = hidden.shape[1]

        def near_copy(by):
            to = lax.rem(part + by, parts)
            return pltpu.make_async_remote_copy(
                src_ref=near_out.at[to], dst_ref=near_in.at[by - 1],
                send_sem=nsend.at[by - 1], recv_sem=nrecv.at[by - 1],
                device_id={"dp": to}, device_id_type=MESH,
            )

        def far_copy(by):
            to = lax.rem(seg + by, count)
            return copy(far_out.at[to], far_in.at[by - 1], wsend.at[by - 1], wrecv.at[by - 1], to)

        def begin():
            logit_grad = jnp.concatenate([dlogit_ref[h] for h in some], axis=1)
            whole_ref[:, model:] = jnp.zeros_like(whole_ref[:, model:])
            whole_ref[:, :model] = lax.dot_general(
                left_t(logit_grad), hidden, (((0,), (0,)), ((), ())), preferred_element_type=F32
            )
            for p in range(parts):
                for c in range(count):
                    at = (p * count + c) * owned
                    near_out[p, c] = whole_ref[:, at:at + breadth]
            for by in range(1, parts):
                near_copy(by).start()

        def middle():
            total = near_out[part]
            for by in range(1, parts):
                near_copy(by).wait_recv()
                total = total + near_in[by - 1]
            far_out[...] = total
            for by in range(1, count):
                far_copy(by).start()

        def end():
            total = far_out[seg]
            for by in range(1, count):
                far_copy(by).wait_recv()
                total = total + far_in[by - 1]
            for by in range(1, parts):
                near_copy(by).wait_send()
            for by in range(1, count):
                far_copy(by).wait_send()
            return total[:, :owned]

        return begin, middle, end

    def heads_of(some):
        return [n for n in some] + [turns + n for n in some]

    cut = turns - 2
    early_begin, early_middle, early_end = reduction(heads_of(range(cut)), *early)
    late_begin, late_middle, late_end = reduction(heads_of(range(cut, turns)), *late)

    lax.fori_loop(0, turns + grad_lag, step, 0)
    late_middle()
    lax.fori_loop(0, turns, drain, 0)
    most = early_end()
    few = late_end()
    weight_ref[...] = stack(most[:cut], few[:2], most[cut:], few[2:])


def move_kernel(*refs):
    half = len(refs) // 2
    sems = refs[-1]
    copies = [pltpu.make_async_copy(refs[n], refs[half + n], sems.at[n]) for n in range(half)]
    for move in copies:
        move.start()
    for move in copies:
        move.wait()


def local(
    queries, key_rows, value_rows, hidden_in, beta_weight, log_gate, out_grad,
    lengths, rewards, prompts,
):
    tokens = queries.shape[0]
    heads = beta_weight.shape[1]
    width = queries.shape[1] // heads
    ctx_count = lax.axis_size("ctx")
    turns = heads // 2
    square = (turns, 2, tokens, tokens)
    states = (turns, width, width)
    pairs = (turns, 2, width, width)
    vmem = pl.BlockSpec(memory_space=pltpu.VMEM)
    hbm = pl.BlockSpec(memory_space=pltpu.HBM)
    model = hidden_in.shape[1]
    dp_count = lax.axis_size("dp")
    owned = model // (dp_count * ctx_count)
    breadth = -(-owned // 128) * 128
    out_shape = (
        jax.ShapeDtypeStruct(queries.shape, BF16),
        jax.ShapeDtypeStruct(queries.shape, BF16),
        jax.ShapeDtypeStruct(queries.shape, BF16),
        jax.ShapeDtypeStruct((heads, tokens), F32),
        jax.ShapeDtypeStruct((heads, owned), F32),
    )

    def reduction_scratch(some):
        return [
            pltpu.VMEM((some, model + breadth), F32),
            pltpu.VMEM((dp_count, ctx_count, some, breadth), F32),
            pltpu.VMEM((dp_count - 1 or 1, ctx_count, some, breadth), F32),
            pltpu.VMEM((ctx_count, some, breadth), F32),
            pltpu.VMEM((ctx_count - 1, some, breadth), F32),
            pltpu.SemaphoreType.DMA((dp_count,)),
            pltpu.SemaphoreType.DMA((dp_count,)),
            pltpu.SemaphoreType.DMA((ctx_count,)),
            pltpu.SemaphoreType.DMA((ctx_count,)),
        ]

    grads = pl.pallas_call(
        kernel,
        out_shape=out_shape,
        in_specs=[hbm] * 10,
        out_specs=(vmem,) * 5,
        scratch_shapes=[
            pltpu.SMEM(lengths.shape, jnp.int32),
            pltpu.SMEM(rewards.shape, F32),
            pltpu.SMEM(prompts.shape, jnp.int32),
        ]
        + [pltpu.VMEM(queries.shape, BF16)] * 4
        + [
            pltpu.VMEM(hidden_in.shape, BF16),
            pltpu.VMEM((heads, model), BF16),
            pltpu.VMEM(log_gate.shape, F32),
            pltpu.VMEM((heads, tokens, 4), F32),
            pltpu.VMEM((heads, 2, tokens), F32),
            pltpu.SemaphoreType.DMA((10,)),
        ]
        + [pltpu.VMEM(square, F32)] * 4
        + [
            pltpu.VMEM((turns, 2, 3, width, width), F32),
            pltpu.VMEM((turns, 3, width, width), F32),
            pltpu.VMEM((turns, 3, width, width), F32),
        ]
        + [pltpu.VMEM(pairs, F32)] * 2
        + [pltpu.VMEM(states, F32)] * 4
        + [
            pltpu.VMEM((heads, tokens, 1), F32),
        ]
        + [pltpu.SemaphoreType.DMA((turns,))] * 12
        + reduction_scratch(heads - 4)
        + reduction_scratch(4),
        compiler_params=pltpu.CompilerParams(
            collective_id=0, has_side_effects=True, vmem_limit_bytes=48 * 2**20
        ),
        name="delta_backward",
    )(
        *[pltpu.with_memory_space_constraint(x, pltpu.HBM) for x in (
            lengths, rewards, prompts,
            queries, key_rows, value_rows, out_grad, hidden_in, beta_weight.T, log_gate,
        )],
    )
    dq, dk, dv, dgate, own_grad = pl.pallas_call(
        move_kernel,
        out_shape=out_shape,
        in_specs=[vmem] * 5,
        out_specs=(hbm,) * 5,
        scratch_shapes=[pltpu.SemaphoreType.DMA((5,))],
        compiler_params=pltpu.CompilerParams(vmem_limit_bytes=4 * 2**20),
        name="store_grads",
    )(*grads)
    return (dq, dk, dv, dgate, own_grad.T)


def solution(mesh):
    rows = P(("dp", "ctx"), None)
    in_specs = (
        rows, rows, rows, rows, P(), P(None, ("dp", "ctx")), rows, P("dp", None), P(), P(),
    )
    out_specs = (rows, rows, rows, P(None, ("dp", "ctx")), rows)
    return jax.shard_map(local, mesh=mesh, in_specs=in_specs, out_specs=out_specs, check_vma=False)
```

```python
import functools

import jax
import jax.numpy as jnp
from jax import lax
from jax.experimental import pallas as pl
from jax.experimental.pallas import tpu as pltpu
from jax.sharding import PartitionSpec as P

SMALL = 16
MAP_LAG = 2
GRAD_SLACK = 1
DETOUR_LAG = 2
MANY = (0, 2, 4)
FEW = (2,)
EXTRA = (3,)
MESH = pl.DeviceIdType.MESH
F32 = jnp.float32
BF16 = jnp.bfloat16


def split(x):
    hi = x.astype(BF16)
    return hi, (x - hi.astype(F32)).astype(BF16)


def left(x):
    return jnp.concatenate(split(x), axis=1)


def left_t(x):
    return jnp.concatenate(split(x), axis=0)


def right(x):
    row = jnp.concatenate(split(x), axis=1)
    return jnp.concatenate([row, row], axis=0)


def right_t(x):
    hi, lo = split(x)
    return jnp.concatenate(
        [jnp.concatenate([hi, hi], axis=1), jnp.concatenate([lo, lo], axis=1)], axis=0
    )


def contract(a, b, dims):
    out = lax.dot_general(a, b, ((dims[:1], dims[1:]), ((), ())), preferred_element_type=F32)
    half = out.shape[1] // 2
    return out[:, :half] + out[:, half:]


def mul(a, b):
    return contract(left(a), right(b), (1, 0))


def mul_t(a, b):
    return contract(left(a), right_t(b), (1, 1))


def t_mul(a, b):
    return contract(left_t(a), right(b), (0, 0))


def stack(*parts):
    return jnp.concatenate(parts, axis=0)


def row_sum(x):
    return jnp.sum(x, axis=1, keepdims=True)


def inverses(lows, rows, cols):
    size = lows[0].shape[0]
    eye = jnp.where(rows == cols, 1.0, 0.0)
    base = min(SMALL, size)
    same = (rows // base) == (cols // base)
    powers = [jnp.where(same, -low, 0.0) for low in lows]
    totals = [eye + power for power in powers]
    powers = [mul(power, power) for power in powers]
    reach = 2
    while reach * 2 < base:
        both = [mul(stack(t, p), p) for t, p in zip(totals, powers)]
        totals = [t + b[:size] for t, b in zip(totals, both)]
        powers = [b[size:] for b in both]
        reach *= 2
    totals = [t + mul(t, p) for t, p in zip(totals, powers)]
    while base < size:
        own = ((rows // (2 * base)) == (cols // (2 * base))) & ((rows // base) != (cols // base))
        parts = [jnp.where(own, low, 0.0) for low in lows]
        mids = [mul(t, part) for t, part in zip(totals, parts)]
        totals = [t - mul(m, t) for t, m in zip(totals, mids)]
        base *= 2
    return totals


def kernel(
    length_in, reward_in, prompt_in,
    q_in, k_in, v_in, o_in, hidden_in, proj_in, gate_in,
    dq_ref, dk_ref, dv_ref, dgate_ref, weight_ref,
    length_ref, reward_ref, prompt_ref,
    q_ref, k_ref, v_ref, o_ref, hidden_ref, proj_ref, gate_ref, cols_ref, rows_ref, table_ref, wide_ref, load_sem,
    inv_ref, mix_ref, dkk_ref, dec_ref, maps_ref, give_ref,
    detour_ref, fpair_ref, bpair_ref, fout_ref, bout_ref, fmate_ref, bmate_ref,
    dlogit_ref,
    msend, mrecv, fsend, frecv, bsend, brecv, fgive, ftake, bgive, btake,
    dsend, drecv, *sums,
):
    early, late = sums[:len(sums) // 2], sums[len(sums) // 2:]
    tokens = q_ref.shape[0]
    width = fout_ref.shape[-1]
    turns = fout_ref.shape[0]
    count = lax.axis_size("ctx")
    seg = lax.axis_index("ctx")
    tiers = count // 2
    tier = seg // 2
    side = lax.rem(seg, 2)
    owned = weight_ref.shape[1]
    breadth = wide_ref.shape[1] // (lax.axis_size("dp") * count)
    mate = seg + 1 - 2 * side

    loads = [
        pltpu.make_async_copy(src, dst, load_sem.at[n])
        for n, (src, dst) in enumerate([
            (length_in, length_ref), (reward_in, reward_ref), (prompt_in, prompt_ref),
            (gate_in, gate_ref), (proj_in, proj_ref), (hidden_in, hidden_ref), (k_in, k_ref),
            (q_in, q_ref), (v_in, v_ref), (o_in, o_ref),
        ])
    ]
    for load_copy in loads:
        load_copy.start()

    barrier = pltpu.get_barrier_semaphore()

    part = lax.axis_index("dp")
    parts = lax.axis_size("dp")
    for by in range(1, count):
        pl.semaphore_signal(
            barrier, inc=1, device_id={"ctx": lax.rem(seg + by, count)}, device_id_type=MESH
        )
    for by in range(1, parts):
        pl.semaphore_signal(
            barrier, inc=1, device_id={"dp": lax.rem(part + by, parts)}, device_id_type=MESH
        )

    rows = lax.broadcasted_iota(jnp.int32, (tokens, tokens), 0)
    cols = lax.broadcasted_iota(jnp.int32, (tokens, tokens), 1)

    for load_copy in loads[:3]:
        load_copy.wait()
    rolls = length_ref.shape[1]
    amounts = []
    for i in range(rolls):
        own = prompt_ref[part * rolls + i]
        total, members = jnp.zeros((1, tokens), F32), jnp.zeros((1, tokens), F32)
        for j in range(reward_ref.shape[0]):
            same = jnp.where(prompt_ref[j] == own, 1.0, 0.0)
            total = total + same * reward_ref[j]
            members = members + same
        advantage = reward_ref[part * rolls + i] - total / members
        length = jnp.zeros((1, tokens), F32) + length_ref[0, i].astype(F32)
        amounts.append(advantage * (tokens * count) / (rolls * length))

    def plan(spots, spread_out):
        number, weight = jnp.zeros(spots.shape, F32), jnp.zeros(spots.shape, F32)
        begin = 0
        for i in range(rolls):
            end = begin + length_ref[0, i]
            started = (spots >= begin) & (begin >= seg * tokens)
            number = number + jnp.where(started, 1.0, 0.0)
            amount = spread_out(amounts[i])
            weight = weight + jnp.where((spots >= begin) & (spots < end), amount, 0.0)
            begin = end
        return number, weight

    number_row, _ = plan(seg * tokens + cols[:1, :], lambda x: x)
    number_col, weight_col = plan(seg * tokens + rows[:, :1], lambda x: x[:, :1])

    def thirds(x):
        first = x.astype(BF16)
        rest = x - first.astype(F32)
        second = rest.astype(BF16)
        return first, second, (rest - second.astype(F32)).astype(BF16)

    loads[3].wait()
    upto = jnp.where(rows <= cols, 1.0, 0.0).astype(BF16)
    gates = jnp.concatenate(thirds(gate_ref[...]), axis=0)
    heads_all = gate_ref.shape[0]
    sums = lax.dot_general(gates, upto, (((1,), (0,)), ((), ())), preferred_element_type=F32)
    gamma_rows = (sums[2 * heads_all:] + sums[heads_all:2 * heads_all]) + sums[:heads_all]
    for h in range(heads_all):
        rows_ref[h] = jnp.concatenate([gamma_rows[h:h + 1], number_row], axis=0)
    gamma_cols = gamma_rows.T
    loads[4].wait()
    loads[5].wait()
    logits = lax.dot_general(
        hidden_ref[...], proj_ref[...], (((1,), (1,)), ((), ())), preferred_element_type=F32
    )
    betas = jax.nn.sigmoid(logits)
    turn_count = heads_all // 2
    table_ref[0] = betas
    table_ref[1] = gamma_cols
    table_ref[2, :, :2] = jnp.concatenate([number_col, weight_col], axis=1)

    def write_columns(some):
        shared = table_ref[2, :, :2]
        for h in some:
            cols_ref[h] = jnp.concatenate(
                [table_ref[0, :, h:h + 1], table_ref[1, :, h:h + 1], shared], axis=1
            )

    write_columns((0, turn_count))
    for load_copy in loads[6:]:
        load_copy.wait()
    pl.semaphore_wait(barrier, count + parts - 2)

    def copy(src, dst, sent, landed, to):
        return pltpu.make_async_remote_copy(
            src_ref=src, dst_ref=dst, send_sem=sent, recv_sem=landed,
            device_id={"ctx": to}, device_id_type=MESH,
        )

    first_tier, last_tier = tier == 0, tier == tiers - 1
    low, high = side == 0, side == 1
    sends_one = (first_tier & low) | (last_tier & high)
    takes_one = (first_tier & high) | (last_tier & low)

    def among(i, some):
        return functools.reduce(jnp.logical_or, [i == n for n in some])

    lower_mid, upper_mid = tier == 1, tier == tiers - 2

    def goes_down(i):
        edge = lower_mid & ((low & among(i, MANY)) | (high & among(i, FEW)))
        return (tiers >= 4) & (edge | (upper_mid & low & among(i, EXTRA)))

    def goes_up(i):
        edge = upper_mid & ((high & among(i, MANY)) | (low & among(i, FEW)))
        return (tiers >= 4) & (edge | (lower_mid & high & among(i, EXTRA)))

    def passes_up(i):
        edge = first_tier & ((high & among(i, MANY)) | (low & among(i, FEW)))
        return (tiers >= 4) & (edge | ((tier == tiers - 3) & high & among(i, EXTRA)))

    def passes_down(i):
        edge = last_tier & ((low & among(i, MANY)) | (high & among(i, FEW)))
        return (tiers >= 4) & (edge | ((tier == 2) & low & among(i, EXTRA)))

    def map_copy(i):
        return copy(give_ref.at[i], maps_ref.at[i, side], msend.at[i], mrecv.at[i], mate)

    def one_copy(i):
        return copy(
            give_ref.at[i, 1 + side], maps_ref.at[i, side, 1 + side], msend.at[i], mrecv.at[i],
            mate,
        )

    def detour_copy(i):
        via = mate + jnp.where(goes_down(i), -2, 2)
        return copy(give_ref.at[i], detour_ref.at[i], msend.at[i], drecv.at[i], via)

    def pass_copy(i):
        to = seg + jnp.where(passes_up(i), 2, -2)
        return copy(detour_ref.at[i], maps_ref.at[i, 1 - side], dsend.at[i], mrecv.at[i], to)

    def forward_copy(i):
        return copy(fout_ref.at[i], fpair_ref.at[i, 0], fsend.at[i], frecv.at[i], seg + 2)

    def backward_copy(i):
        return copy(bout_ref.at[i], bpair_ref.at[i, 1], bsend.at[i], brecv.at[i], seg - 2)

    def state_copy(i):
        return copy(fpair_ref.at[i, 1 - side], fmate_ref.at[i], fgive.at[i], ftake.at[i], mate)

    def after_copy(i):
        return copy(bpair_ref.at[i, 1 - side], bmate_ref.at[i], bgive.at[i], btake.at[i], mate)

    both_heads = range(2)

    def head_of(turn, j):
        return (side if j == 0 else 1 - side) * turns + turn

    def lanes(h):
        return pl.ds(pl.multiple_of(h * width, width), width)

    def load(ref, h):
        return ref[:, lanes(h)].astype(F32)

    def token_columns(h):
        block = cols_ref[h]
        row_block = rows_ref[h]
        beta, gamma = block[:, 0:1], block[:, 1:2]
        number, weight = block[:, 2:3], block[:, 3:4]
        gamma_row, number_row = row_block[0:1, :], row_block[1:2, :]
        head = jnp.where(number == 0.0, jnp.exp(gamma), 0.0)
        tied = number == number_row[:, tokens - 1:tokens]
        tail = jnp.where(
            tied, jnp.exp(jnp.where(tied, gamma_row[:, tokens - 1:tokens] - gamma, 0.0)), 0.0
        )
        return beta, gamma, number, weight, gamma_row, number_row, head, tail

    def scales(x):
        return lax.rsqrt(row_sum(x * x) + 1e-06)

    def local_part(turn):
        lows, keep = [], []
        for j in both_heads:
            h = head_of(turn, j)
            beta, gamma, number, weight, gamma_row, number_row, head, tail = token_columns(h)
            q, k = load(q_ref, h), load(k_ref, h)
            qh, kh = q * scales(q), k * scales(k)
            linked = (number == number_row) & (rows >= cols)
            decay = jnp.where(linked, jnp.exp(jnp.where(linked, gamma - gamma_row, 0.0)), 0.0)
            both = mul_t(stack(kh, qh), kh)
            dkk = jnp.where(rows > cols, decay * both[:tokens], 0.0)
            mix = decay * both[tokens:]
            dec_ref[turn, j] = decay
            dkk_ref[turn, j] = dkk
            mix_ref[turn, j] = mix
            lows.append(beta * dkk)
            keep.append((h, beta, weight, head, tail, qh, kh, mix))
        invs = inverses(lows, rows, cols)
        for j in both_heads:
            inv_ref[turn, j] = invs[j]
        pairs = []
        for j in both_heads:
            h, beta, weight, head, tail, qh, kh, mix = keep[j]
            v = load(v_ref, h)
            pairs.append(mul(invs[j], jnp.concatenate([beta * v, (beta * head) * kh], axis=1)))
        eye = jnp.where(rows == cols, 1.0, 0.0)
        for j in both_heads:
            h, beta, weight, head, tail, qh, kh, mix = keep[j]
            out = maps_ref.at[turn, side] if j == 0 else give_ref.at[turn]
            z = pairs[j][:, width:]
            ends = t_mul(pairs[j], tail * kh)
            out[0] = head[tokens - 1:tokens, :] * eye - ends[width:]
            out[1] = ends[:width]
            carry = head * qh - mul(mix, z)
            out[2] = t_mul(load(o_ref, h) * weight, carry)

    def forward_step(i):
        @pl.when(first_tier)
        def _():
            fpair_ref[i, 0] = jnp.zeros((width, width), F32)
            fpair_ref[i, 1] = maps_ref[i, 0, 1]

        @pl.when(jnp.logical_not(first_tier))
        def _():
            forward_copy(i).wait_recv()
            fpair_ref[i, 1] = mul(fpair_ref[i, 0], maps_ref[i, 0, 0]) + maps_ref[i, 0, 1]

        @pl.when(jnp.logical_not(last_tier))
        def _():
            fout_ref[i] = mul(fpair_ref[i, 1], maps_ref[i, 1, 0]) + maps_ref[i, 1, 1]
            forward_copy(i).start()

        @pl.when(jnp.logical_not(first_tier & high))
        def _():
            state_copy(i).start()

    def backward_step(i):
        @pl.when(last_tier)
        def _():
            bpair_ref[i, 1] = jnp.zeros((width, width), F32)
            bpair_ref[i, 0] = maps_ref[i, 1, 2]

        @pl.when(jnp.logical_not(last_tier))
        def _():
            backward_copy(i).wait_recv()
            bpair_ref[i, 0] = mul_t(bpair_ref[i, 1], maps_ref[i, 1, 0]) + maps_ref[i, 1, 2]

        @pl.when(jnp.logical_not(first_tier))
        def _():
            bout_ref[i] = mul_t(bpair_ref[i, 0], maps_ref[i, 0, 0]) + maps_ref[i, 0, 2]
            backward_copy(i).start()

        @pl.when(jnp.logical_not(last_tier & low))
        def _():
            after_copy(i).start()

    def gradient_first(turn):
        @pl.when(first_tier & low)
        def _():
            fmate_ref[turn] = jnp.zeros((width, width), F32)

        @pl.when(jnp.logical_not(first_tier & low))
        def _():
            state_copy(turn).wait_recv()

        @pl.when(last_tier & high)
        def _():
            bmate_ref[turn] = jnp.zeros((width, width), F32)

        @pl.when(jnp.logical_not(last_tier & high))
        def _():
            after_copy(turn).wait_recv()

        upper = jnp.where(rows < cols, 1.0, 0.0).astype(BF16)
        upper = stack(upper, upper)
        keep = []
        afters = [bpair_ref[turn, side], bmate_ref[turn]]
        for j in both_heads:
            h = head_of(turn, j)
            beta, gamma, number, weight, gamma_row, number_row, head, tail = token_columns(h)
            q, k = load(q_ref, h), load(k_ref, h)
            qs, ks = scales(q), scales(k)
            qh, kh = q * qs, k * ks
            state = fpair_ref[turn, side] if j == 0 else fmate_ref[turn]
            both = mul_t(stack(qh, kh), state)
            keep.append((beta, weight, head, tail, qs, ks, qh, kh, state, both[:tokens], both[tokens:]))
        heads = [head_of(turn, j) for j in both_heads]
        rests = [load(v_ref, heads[i]) - keep[i][2] * keep[i][10] for i in both_heads]
        us = [mul(inv_ref[turn, i], keep[i][0] * rests[i]) for i in both_heads]
        dos = [load(o_ref, heads[i]) * keep[i][1] for i in both_heads]
        dus = [
            t_mul(mix_ref[turn, i], dos[i]) + mul_t(keep[i][3] * keep[i][7], afters[i])
            for i in both_heads
        ]
        drs = [t_mul(inv_ref[turn, i], dus[i]) for i in both_heads]
        squares = [mul_t(stack(dos[i], drs[i]), us[i]) for i in both_heads]
        lows = []
        for i in both_heads:
            beta = keep[i][0]
            dlow = jnp.where(rows > cols, -squares[i][tokens:], 0.0)
            lowpart = dlow * dkk_ref[turn, i]
            dbeta = row_sum(drs[i] * rests[i]) + row_sum(lowpart)
            dlogit_ref[heads[i]] = dbeta * beta * (1.0 - beta)
            lows.append((dlow, lowpart))
        return upper, keep, afters, heads, us, dos, drs, squares, lows

    def gradient_rest(turn, values):
        upper, keep, afters, heads, us, dos, drs, squares, lows = values
        for i in both_heads:
            beta, weight, head, tail, qs, ks, qh, kh, state, qstate, kstate = keep[i]
            h = heads[i]
            u, do, dr, after = us[i], dos[i], drs[i], afters[i]
            decay = dec_ref[turn, i]
            dlow, lowpart = lows[i]
            dmix = squares[i][:tokens]
            inward = mul(stack(head * do, (-beta * head) * dr), state)
            uafter = mul(u, after)
            da = dmix * decay
            dpair = dlow * (beta * decay)
            pairs = stack(da, dpair)
            direct = mul(pairs, kh)
            turned = t_mul(pairs, stack(qh, kh))
            dqh = inward[:tokens] + direct[:tokens]
            dkh = inward[tokens:] + direct[tokens:] + turned + tail * uafter
            dq_ref[:, lanes(h)] = (qs * (dqh - qh * row_sum(qh * dqh))).astype(BF16)
            dk_ref[:, lanes(h)] = (ks * (dkh - kh * row_sum(kh * dkh))).astype(BF16)
            dv_ref[:, lanes(h)] = (beta * dr).astype(BF16)
            spread = dmix * mix_ref[turn, i] + beta * lowpart
            across = lax.dot_general(
                left(spread), upper, (((1,), (0,)), ((), ())), preferred_element_type=F32
            )
            total = jnp.sum(row_sum(after * state), axis=0, keepdims=True)
            headgrad = row_sum(do * qstate) - beta * row_sum(dr * kstate)
            headgrad = head * (headgrad + jnp.where(rows[:, :1] == tokens - 1, total, 0.0))
            tailgrad = tail * row_sum(kh * uafter)
            dgate_ref[pl.ds(h, 1), :] = jnp.sum(
                jnp.where(rows >= cols, across + headgrad, tailgrad), axis=0, keepdims=True
            )

    def within(i):
        return (i >= 0) & (i < turns)

    grad_lag = MAP_LAG + tiers + GRAD_SLACK

    def step(t, unused):
        @pl.when(t < turns)
        def _():
            local_part(t)
            detour = goes_down(t) | goes_up(t)

            @pl.when(sends_one)
            def _():
                one_copy(t).start()

            @pl.when(detour)
            def _():
                detour_copy(t).start()

            @pl.when(jnp.logical_not(sends_one | detour))
            def _():
                map_copy(t).start()

        @pl.when(t == 0)
        def _():
            write_columns([h for h in range(heads_all) if h not in (0, turn_count)])

        @pl.when(t == 1)
        def _():
            wide_ref[...] = jnp.zeros_like(wide_ref)
            for n in range(parts * count):
                wide_ref[:, n * breadth:n * breadth + owned] = (
                    hidden_ref[:, n * owned:(n + 1) * owned]
                )

        d = t - DETOUR_LAG

        @pl.when(within(d) & (passes_up(d) | passes_down(d)))
        def _():
            detour_copy(d).wait_recv()
            pass_copy(d).start()

        f = t - MAP_LAG - tier
        b = t - MAP_LAG - (tiers - 1 - tier)
        m = jnp.maximum(f, b)

        @pl.when(within(m))
        def _():
            @pl.when(takes_one)
            def _():
                one_copy(m).wait_recv()

            @pl.when(jnp.logical_not(takes_one))
            def _():
                map_copy(m).wait_recv()

        @pl.when(within(f))
        def _():
            forward_step(f)

        @pl.when(within(b))
        def _():
            backward_step(b)

        @pl.when(within(t - grad_lag))
        def _():
            g = t - grad_lag

            @pl.when(g == cut)
            def _():
                early_begin()

            values = gradient_first(g)

            @pl.when(g == turns - 1)
            def _():
                late_begin()

            gradient_rest(g, values)

            @pl.when(g == cut)
            def _():
                early_middle()

        return unused


    def drain(i, unused):
        @pl.when(sends_one)
        def _():
            one_copy(i).wait_send()

        @pl.when(jnp.logical_not(sends_one))
        def _():
            map_copy(i).wait_send()

        @pl.when(passes_up(i) | passes_down(i))
        def _():
            pass_copy(i).wait_send()

        @pl.when(jnp.logical_not(first_tier & high))
        def _():
            state_copy(i).wait_send()

        @pl.when(jnp.logical_not(last_tier & low))
        def _():
            after_copy(i).wait_send()

        @pl.when(jnp.logical_not(last_tier))
        def _():
            forward_copy(i).wait_send()

        @pl.when(jnp.logical_not(first_tier))
        def _():
            backward_copy(i).wait_send()

        return unused

    def reduction(some, near_out, near_in, far_out, far_in, nsend, nrecv, wsend, wrecv):
        def near_copy(by):
            to = lax.rem(part + by, parts)
            return pltpu.make_async_remote_copy(
                src_ref=near_out.at[to], dst_ref=near_in.at[by - 1],
                send_sem=nsend.at[by - 1], recv_sem=nrecv.at[by - 1],
                device_id={"dp": to}, device_id_type=MESH,
            )

        def far_copy(by):
            to = lax.rem(seg + by, count)
            return copy(far_out.at[to], far_in.at[by - 1], wsend.at[by - 1], wrecv.at[by - 1], to)

        def begin():
            logit_grad = jnp.concatenate([dlogit_ref[h] for h in some], axis=1)
            wide = wide_ref[...]
            sums = lax.dot_general(
                left_t(logit_grad), stack(wide, wide), (((0,), (0,)), ((), ())),
                preferred_element_type=F32,
            )
            for p in range(parts):
                for c in range(count):
                    at = (p * count + c) * breadth
                    near_out[p, c] = sums[:, at:at + breadth]
            for by in range(1, parts):
                near_copy(by).start()

        def middle():
            total = near_out[part]
            for by in range(1, parts):
                near_copy(by).wait_recv()
                total = total + near_in[by - 1]
            far_out[...] = total
            for by in range(1, count):
                far_copy(by).start()

        def end():
            total = far_out[seg]
            for by in range(1, count):
                far_copy(by).wait_recv()
                total = total + far_in[by - 1]
            for by in range(1, parts):
                near_copy(by).wait_send()
            for by in range(1, count):
                far_copy(by).wait_send()
            return total[:, :owned]

        return begin, middle, end

    def heads_of(some):
        return [n for n in some] + [turns + n for n in some]

    cut = turns - 2
    early_begin, early_middle, early_end = reduction(heads_of(range(cut)), *early)
    late_begin, late_middle, late_end = reduction(heads_of(range(cut, turns)), *late)

    lax.fori_loop(0, turns + grad_lag, step, 0)
    late_middle()
    lax.fori_loop(0, turns, drain, 0)
    most = early_end()
    few = late_end()
    weight_ref[...] = stack(most[:cut], few[:2], most[cut:], few[2:])


def move_kernel(*refs):
    half = len(refs) // 2
    sems = refs[-1]
    copies = [pltpu.make_async_copy(refs[n], refs[half + n], sems.at[n]) for n in range(half)]
    for move in copies:
        move.start()
    for move in copies:
        move.wait()


def local(
    queries, key_rows, value_rows, hidden_in, beta_weight, log_gate, out_grad,
    lengths, rewards, prompts,
):
    tokens = queries.shape[0]
    heads = beta_weight.shape[1]
    width = queries.shape[1] // heads
    ctx_count = lax.axis_size("ctx")
    turns = heads // 2
    square = (turns, 2, tokens, tokens)
    states = (turns, width, width)
    pairs = (turns, 2, width, width)
    vmem = pl.BlockSpec(memory_space=pltpu.VMEM)
    hbm = pl.BlockSpec(memory_space=pltpu.HBM)
    model = hidden_in.shape[1]
    dp_count = lax.axis_size("dp")
    owned = model // (dp_count * ctx_count)
    breadth = -(-owned // 128) * 128
    out_shape = (
        jax.ShapeDtypeStruct(queries.shape, BF16),
        jax.ShapeDtypeStruct(queries.shape, BF16),
        jax.ShapeDtypeStruct(queries.shape, BF16),
        jax.ShapeDtypeStruct((heads, tokens), F32),
        jax.ShapeDtypeStruct((heads, owned), F32),
    )

    def reduction_scratch(some):
        return [
            pltpu.VMEM((dp_count, ctx_count, some, breadth), F32),
            pltpu.VMEM((dp_count - 1 or 1, ctx_count, some, breadth), F32),
            pltpu.VMEM((ctx_count, some, breadth), F32),
            pltpu.VMEM((ctx_count - 1, some, breadth), F32),
            pltpu.SemaphoreType.DMA((dp_count,)),
            pltpu.SemaphoreType.DMA((dp_count,)),
            pltpu.SemaphoreType.DMA((ctx_count,)),
            pltpu.SemaphoreType.DMA((ctx_count,)),
        ]

    grads = pl.pallas_call(
        kernel,
        out_shape=out_shape,
        in_specs=[hbm] * 10,
        out_specs=(vmem,) * 5,
        scratch_shapes=[
            pltpu.SMEM(lengths.shape, jnp.int32),
            pltpu.SMEM(rewards.shape, F32),
            pltpu.SMEM(prompts.shape, jnp.int32),
        ]
        + [pltpu.VMEM(queries.shape, BF16)] * 4
        + [
            pltpu.VMEM(hidden_in.shape, BF16),
            pltpu.VMEM((heads, model), BF16),
            pltpu.VMEM(log_gate.shape, F32),
            pltpu.VMEM((heads, tokens, 4), F32),
            pltpu.VMEM((heads, 2, tokens), F32),
            pltpu.VMEM((3, tokens, heads), F32),
            pltpu.VMEM((tokens, dp_count * ctx_count * breadth), BF16),
            pltpu.SemaphoreType.DMA((10,)),
        ]
        + [pltpu.VMEM(square, F32)] * 4
        + [
            pltpu.VMEM((turns, 2, 3, width, width), F32),
            pltpu.VMEM((turns, 3, width, width), F32),
            pltpu.VMEM((turns, 3, width, width), F32),
        ]
        + [pltpu.VMEM(pairs, F32)] * 2
        + [pltpu.VMEM(states, F32)] * 4
        + [
            pltpu.VMEM((heads, tokens, 1), F32),
        ]
        + [pltpu.SemaphoreType.DMA((turns,))] * 12
        + reduction_scratch(heads - 4)
        + reduction_scratch(4),
        compiler_params=pltpu.CompilerParams(
            collective_id=0, has_side_effects=True, vmem_limit_bytes=48 * 2**20
        ),
        name="delta_backward",
    )(
        *[pltpu.with_memory_space_constraint(x, pltpu.HBM) for x in (
            lengths, rewards, prompts,
            queries, key_rows, value_rows, out_grad, hidden_in, beta_weight.T, log_gate,
        )],
    )
    dq, dk, dv, dgate, own_grad = pl.pallas_call(
        move_kernel,
        out_shape=out_shape,
        in_specs=[vmem] * 5,
        out_specs=(hbm,) * 5,
        scratch_shapes=[pltpu.SemaphoreType.DMA((5,))],
        compiler_params=pltpu.CompilerParams(vmem_limit_bytes=4 * 2**20),
        name="store_grads",
    )(*grads)
    return (dq, dk, dv, dgate, own_grad.T)


def solution(mesh):
    rows = P(("dp", "ctx"), None)
    in_specs = (
        rows, rows, rows, rows, P(), P(None, ("dp", "ctx")), rows, P("dp", None), P(), P(),
    )
    out_specs = (rows, rows, rows, P(None, ("dp", "ctx")), rows)
    return jax.shard_map(local, mesh=mesh, in_specs=in_specs, out_specs=out_specs, check_vma=False)
```
